128 devices in a mesh: row: 8 (over x, core), col: 8 (over z_lo, y), mom: 2 (over z_hi).
Axes of the slice: x: 4, y: 4, z: 4 (z_hi: 2, z_lo: 2; z = z_hi * 2 + z_lo), core: 2. Of those that a mesh axis runs over, the one named last changes fastest.
Arguments:
- lesser: bfloat16 [4, 2, 3072, 3072], P('mom', None, 'row', 'col'), may hold values from -8 to 8
- greater: bfloat16 [4, 2, 3072, 3072], P('mom', None, 'col', 'row'), may hold values from -8 to 8
- triples: int32 [4, 8, 3], replicated, may hold values from 0 to 3
- diag_inverse: bfloat16 [4, 2, 3072, 384], P('mom', None, 'row'), may hold values from -0.21875 to 0.21875
- right_side: bfloat16 [4, 3072, 2, 3072], P('mom', 'row', None, 'col'), may hold values from -6 to 6
Outputs:
- sigma: bfloat16 [4, 2, 3072, 3072], P('mom', None, 'row', 'col')
- solution: bfloat16 [4, 3072, 2, 3072], P('mom', 'row', None, 'col')
The draws below stay inside these ranges and needn't reach their ends.
Inputs may be any that keep to these rules, and one draw needn't show every extreme that they name: `triples`: each entry names a momentum point.
All inputs are finite; a program needn't handle non-finite values.
Results may differ from the reference program's by a relative error of at most 0.017.
Values may be sent and summed in bfloat16 or wider, within the bound.
A program may use at most 128 MiB of HBM per device.

```python
import math
import jax
import jax.numpy as jnp
from jax import lax

PAIRS = 8
K = 4
BO = 384
N = 3072
N_ROW = 8


def place_ends(result, rng, least, top_value):
    shape = result.shape
    index_at = [jax.random.randint(jax.random.fold_in(rng, axis), (), 0, shape[axis]) for axis in range(len(shape))]
    result = result.at[tuple(index_at)].set(least)
    longest = shape.index(max(shape))
    index_at[longest] = (index_at[longest] + 1) % shape[longest]
    return result.at[tuple(index_at)].set(top_value)


def level_of(own_key, extent, cuts, low, high):
    factor_of = 1.0
    for position, parts in cuts:
        draws = jax.random.uniform(jax.random.fold_in(jax.random.fold_in(own_key, 6), position), (parts,), jnp.float32, low / len(cuts), high / len(cuts))
        factor_of = factor_of * jnp.repeat(jnp.exp(draws), extent[position] // parts).reshape((-1,) + (1,) * (len(extent) - 1 - position))
    return factor_of


def gaussian(own_key, extent, spread, bound, pieces=(), held_as=jnp.bfloat16):
    result = spread * jax.random.normal(own_key, extent, jnp.float32)
    if pieces:
        result = result * level_of(own_key, extent, pieces, -0.22, 0.18)
    return jnp.clip(result, -bound, bound).astype(held_as)


def setup_inputs(seed: int = 0) -> dict:
    seeds = jax.random.split(jax.random.key(seed), 6)
    return {
        "lesser": gaussian(seeds[0], (K, 2, N, N), 1.32, 8.0, ((0, 2), (2, 8), (3, 8))),
        "greater": gaussian(seeds[1], (K, 2, N, N), 1.32, 8.0, ((0, 2), (2, 8), (3, 8))),
        "triples": place_ends(jax.random.randint(seeds[2], (K, PAIRS, 3), 0, K), jax.random.fold_in(seeds[2], 1), 0, K - 1).astype(jnp.int32),
        "diag_inverse": gaussian(seeds[3], (K, 2, N, BO), (2 * BO) ** -0.5, 0.21875, ((0, 2), (2, 8))),
        "right_side": gaussian(seeds[4], (K, N, 2, N), 1.0, 6.0, ((0, 2), (1, 8), (3, 8))),
    }


def complex_mul(left_real, left_imag, right_real, right_imag):
    return (left_real * right_real - left_imag * right_imag, left_real * right_imag + left_imag * right_real)

def self_energy(lesser, partner, table_rows):

    def add_term(pair_index, carry):
        sum_real, sum_imag = carry
        first_tile = lax.dynamic_index_in_dim(lesser, table_rows[pair_index, 0], 0, keepdims=False).astype(jnp.float32)
        second_tile = lax.dynamic_index_in_dim(lesser, table_rows[pair_index, 1], 0, keepdims=False).astype(jnp.float32)
        third_tile = lax.dynamic_index_in_dim(partner, table_rows[pair_index, 2], 0, keepdims=False).astype(jnp.float32)
        prod_real, prod_imag = complex_mul(first_tile[0], first_tile[1], second_tile[0], second_tile[1])
        full_real, full_imag = complex_mul(prod_real, prod_imag, third_tile[0], third_tile[1])
        return (sum_real + full_real, sum_imag + full_imag)
    zero_tile = jnp.zeros((N, N), jnp.float32)
    sum_real, sum_imag = lax.fori_loop(0, PAIRS, add_term, (zero_tile, zero_tile))
    return (jnp.stack([sum_real, sum_imag]) * (1.0 / PAIRS)).astype(jnp.bfloat16)

def complex_rows(left_tiles, right_rows):
    left_real = left_tiles[0]
    left_imag = left_tiles[1]
    right_real = right_rows[:, 0, :]
    right_imag = right_rows[:, 1, :]
    out_real = jnp.dot(left_real, right_real, preferred_element_type=jnp.float32) - jnp.dot(left_imag, right_imag, preferred_element_type=jnp.float32)
    out_imag = jnp.dot(left_real, right_imag, preferred_element_type=jnp.float32) + jnp.dot(left_imag, right_real, preferred_element_type=jnp.float32)
    return jnp.stack([out_real, out_imag], axis=1)

def solve_momentum(kernel, inverse, right):
    weight = 1.0 / math.sqrt(N)
    finished = []
    for block in range(N_ROW):
        row_start = block * BO
        row_stop = row_start + BO
        pending = right[row_start:row_stop].astype(jnp.float32)
        if block > 0:
            earlier = jnp.concatenate(finished, axis=0)
            pending = pending + weight * complex_rows(kernel[:, row_start:row_stop, :row_start], earlier)
        rounded = pending.astype(jnp.bfloat16)
        finished.append(complex_rows(inverse[:, row_start:row_stop, :], rounded).astype(jnp.bfloat16))
    return jnp.concatenate(finished, axis=0)

def reference(lesser, greater, triples, diag_inverse, right_side):
    partner = jnp.swapaxes(greater, 2, 3)
    sigma_list = []
    solved_list = []
    for momentum in range(K):
        sigma_one = self_energy(lesser, partner, triples[momentum])
        sigma_list.append(sigma_one)
        solved_list.append(solve_momentum(sigma_one, diag_inverse[momentum], right_side[momentum]))
    return (jnp.stack(sigma_list), jnp.stack(solved_list))
```

```python
import math

import jax
import jax.numpy as jnp
from jax import lax
from jax.experimental import pallas as pl
from jax.experimental.pallas import tpu as pltpu
from jax.sharding import PartitionSpec as P

MESH = pl.DeviceIdType.MESH
SIDE = 384
WIDE = 2 * SIDE
CHUNKS = 3
PART = SIDE // CHUNKS
GROUPS = 3
LANES = 128
PAIRS = 8
SUB = 16


def expand(tall):
    real, imag = tall[:, :LANES], tall[:, LANES:]
    turned = jnp.concatenate([-imag, real], axis=1)
    return jnp.concatenate([tall, turned], axis=0)


def kernel(
    triples, lesser, greater, diag, right,
    sigma, solved,
    l0, l1, l2, g0, g1, g2, partner, own_sigma, rows_of, dbuf, rbuf, acc, sol,
    ex_s, ex_r, loc, zs, zr, ys, yr, ss, sr, rs, rr, dl, ds_, dr, xs, xr, os_, or_, out_s,
):
    lch, gch = (l0, l1, l2), (g0, g1, g2)
    row = lax.axis_index("row")
    col = lax.axis_index("col")
    mom = lax.axis_index("mom")
    x, core = row // 2, row % 2
    zl, y = col // 4, col % 4
    weight = 1.0 / math.sqrt(SIDE * 8)

    def at(x_, core_, y_, zl_):
        return (x_ * 2 + core_, zl_ * 4 + y_, mom)

    pair_dev = (row, col, 1 - mom)
    sibling = at(x, 1 - core, y, zl)
    zflip = at(x, core, y, 1 - zl)

    def y_dev(d):
        return at(x, core, (y + d) % 4, zl)

    def x_dev(d):
        return at(x + d, core, y, zl)

    def remote(src, dst, send, recv, dev):
        return pltpu.make_async_remote_copy(
            src_ref=src, dst_ref=dst, send_sem=send, recv_sem=recv, device_id=dev, device_id_type=MESH
        )

    barrier = pltpu.get_barrier_semaphore()
    peers = [pair_dev, sibling, zflip, at(x, 1 - core, y, 1 - zl)]
    peers += [y_dev(d) for d in (1, 2, 3)]
    peers += [at((x + d) % 4, core, y, zl) for d in (1, 2, 3)]
    for peer in peers:
        pl.semaphore_signal(barrier, inc=1, device_id=peer, device_id_type=MESH)
    pl.semaphore_wait(barrier, len(peers))

    needed = col < row
    early = jnp.logical_or(needed, x == 3)
    late = jnp.logical_not(early)

    def part(i):
        return pl.ds(i * PART, PART)

    mine = pl.ds(2 * mom, 2)

    def exchange(i):
        return (
            remote(lesser.at[:, :, part(i), :], lch[i].at[mine], ex_s.at[i, 0], ex_r.at[i, 0], pair_dev),
            remote(greater.at[:, :, :, part(i)], gch[i].at[mine], ex_s.at[i, 1], ex_r.at[i, 1], pair_dev),
        )

    def keep(i):
        return (
            pltpu.make_async_copy(lesser.at[:, :, part(i), :], lch[i].at[mine], loc.at[i, 0]),
            pltpu.make_async_copy(greater.at[:, :, :, part(i)], gch[i].at[mine], loc.at[i, 1]),
        )

    def start_exchange():
        for i in range(CHUNKS):
            for copy in exchange(i):
                copy.start()

    pl.when(early)(start_exchange)

    def right_self(m):
        return jnp.logical_and(core == zl, zl == m)

    def right_send(m):
        return remote(right.at[m], rbuf.at[core], rs.at[m], rr.at[core], at(x, zl, y, m))

    def right_keep(m):
        return pltpu.make_async_copy(right.at[m], rbuf.at[core], rr.at[core])

    for m in range(2):
        pl.when(right_self(m))(lambda m=m: right_keep(m).start())
        pl.when(jnp.logical_not(right_self(m)))(lambda m=m: right_send(m).start())

    def diag_keep(q):
        return pltpu.make_async_copy(diag.at[zl, q], dbuf.at[core, :, pl.ds(q * SIDE, SIDE)], dl.at[q])

    def diag_send(q):
        return remote(
            diag.at[zl, q], dbuf.at[core, :, pl.ds(q * SIDE, SIDE)], ds_.at[q], dr.at[q], sibling
        )

    for q in range(2):
        diag_keep(q).start()
        diag_send(q).start()
    for i in range(CHUNKS):
        for copy in keep(i):
            copy.start()

    def sigma_out(i, q):
        return pltpu.make_async_copy(
            own_sigma.at[:, part(i), pl.ds(q * SIDE, SIDE)], sigma.at[:, q, part(i), :], out_s.at[i, q]
        )

    def compute_sigma(i):
        for copy in exchange(i):
            copy.wait_recv()
        for copy in keep(i):
            copy.wait()

        def turn(k, carry):
            for q in range(2):
                for b in range(3):
                    rows = pl.ds(b * LANES, LANES)
                    partner[k, q, :, rows] = gch[i][k, q, rows, :].T
            return carry

        lax.fori_loop(0, 4, turn, 0)

        def block(s, carry):
            here = pl.ds(pl.multiple_of(s * SUB, SUB), SUB)
            there = pl.ds(pl.multiple_of(i * PART + s * SUB, SUB), SUB)
            for m in range(2):
                sum_real = jnp.zeros((SUB, SIDE), jnp.float32)
                sum_imag = jnp.zeros((SUB, SIDE), jnp.float32)
                for p in range(PAIRS):
                    base = (2 * mom + m) * (3 * PAIRS) + 3 * p
                    a, b, c = triples[base], triples[base + 1], triples[base + 2]
                    ar = lch[i][a, 0, here, :].astype(jnp.float32)
                    ai = lch[i][a, 1, here, :].astype(jnp.float32)
                    br = lch[i][b, 0, here, :].astype(jnp.float32)
                    bi = lch[i][b, 1, here, :].astype(jnp.float32)
                    cr = partner[c, 0, here, :].astype(jnp.float32)
                    ci = partner[c, 1, here, :].astype(jnp.float32)
                    pr = ar * br - ai * bi
                    pi = ar * bi + ai * br
                    sum_real += pr * cr - pi * ci
                    sum_imag += pr * ci + pi * cr
                sig_real = (sum_real * (1.0 / PAIRS)).astype(jnp.bfloat16)
                sig_imag = (sum_imag * (1.0 / PAIRS)).astype(jnp.bfloat16)
                own_sigma[m, there, 0:SIDE] = sig_real
                own_sigma[m, there, SIDE:WIDE] = sig_imag

                @pl.when(zl == m)
                def _():
                    rows_of[core, col, there, 0:SIDE] = sig_real
                    rows_of[core, col, there, SIDE:WIDE] = sig_imag
            return carry

        lax.fori_loop(0, PART // SUB, block, 0)
        for q in range(2):
            sigma_out(i, q).start()

    def hop(i):
        return remote(
            own_sigma.at[1 - zl, part(i), :], rows_of.at[core, col, part(i), :], zs.at[i], zr.at[i], zflip
        )

    other_col = (1 - zl) * 4 + y
    other_needed = other_col < row

    def hop_in(i):
        tile = rows_of.at[core, other_col, part(i), :]
        return remote(tile, tile, zs.at[i], zr.at[i], zflip)

    def y_send(t, i, d):
        j = col if t == 0 else other_col
        src = own_sigma.at[zl, part(i), :] if t == 0 else rows_of.at[core, j, part(i), :]
        return remote(src, rows_of.at[core, j, part(i), :], ys.at[t, i, d - 1], yr.at[j, i], y_dev(d))

    def side_send(j, i):
        tile = rows_of.at[core, j, part(i), :]
        return remote(tile, tile, ss.at[j, i], sr.at[j, i], sibling)

    def side_own(i):
        return remote(
            own_sigma.at[zl, part(i), :], rows_of.at[core, col, part(i), :], ss.at[col, i], sr.at[col, i], sibling
        )

    def side_in(j, i):
        tile = rows_of.at[1 - core, j, part(i), :]
        return remote(tile, tile, ss.at[j, i], sr.at[j, i], sibling)

    def gathered(i):
        for d in (1, 2, 3):
            for half in range(2):
                j = half * 4 + (y + d) % 4

                @pl.when(j < row)
                def _(j=j):
                    tile = rows_of.at[core, j, part(i), :]
                    remote(tile, tile, ss.at[j, i], yr.at[j, i], sibling).wait_recv()
                    side_send(j, i).start()

    for i in range(CHUNKS):
        @pl.when(early)
        def _(i=i):
            compute_sigma(i)

        @pl.when(needed)
        def _(i=i):
            hop(i).start()
            for d in (1, 3, 2):
                y_send(0, i, d).start()
            side_own(i).start()

        @pl.when(other_needed)
        def _(i=i):
            hop_in(i).wait_recv()
            for d in (1, 3, 2):
                y_send(1, i, d).start()
            side_send(other_col, i).start()

        if i:
            gathered(i - 1)
    gathered(CHUNKS - 1)
    pl.when(late)(start_exchange)

    for q in range(2):
        diag_keep(q).wait()
        dst = dbuf.at[1 - core, :, pl.ds(q * SIDE, SIDE)]
        remote(diag.at[zl, q], dst, ds_.at[q], dr.at[q], sibling).wait_recv()
    for q in range(2):
        from_self = jnp.logical_and(core == q, zl == core)

        @pl.when(from_self)
        def _(q=q):
            pltpu.make_async_copy(right.at[0], rbuf.at[q], rr.at[q]).wait()

        @pl.when(jnp.logical_not(from_self))
        def _(q=q):
            remote(right.at[0], rbuf.at[q], rs.at[0], rr.at[q], sibling).wait_recv()

    def sol_send(q, g, d):
        tile = sol.at[2 * x + q, g]
        return remote(tile, tile, xs.at[q, g, d - 1], xr.at[2 * x + q, g], x_dev(d))

    def out_self(q):
        return jnp.logical_and(core == q, zl == core)

    def out_send(q, g):
        return remote(
            sol.at[2 * x + q, g], solved.at[zl, g], os_.at[q, g], or_.at[zl, g], at(x, q, y, core)
        )

    def out_keep(q, g):
        return pltpu.make_async_copy(sol.at[2 * x + q, g], solved.at[zl, g], or_.at[zl, g])

    def side_wait(j, which):
        @pl.when(core != which)
        def _():
            for i in range(CHUNKS):
                side_in(j, i).wait_recv()

    def group(g, carry):
        for q in range(2):
            acc[q] = rbuf[q, g].astype(jnp.float32)

        def update(step, c):
            for t in range(2):
                j = 2 * step + t
                tile = sol.at[j, g]
                remote(tile, tile, xs.at[0, g, 0], xr.at[j, g], sibling).wait_recv()

                @pl.when(g == 0)
                def _(j=j):
                    side_wait(j, 0)
                    side_wait(j, 1)

                factor = expand(sol[j, g])
                for q in range(2):
                    acc[q] += weight * jnp.dot(
                        rows_of[q, j], factor, preferred_element_type=jnp.float32
                    )
            return c

        lax.fori_loop(0, x, update, 0)

        for q in range(2):
            answer = jnp.dot(
                dbuf[q], expand(acc[q].astype(jnp.bfloat16)), preferred_element_type=jnp.float32
            ).astype(jnp.bfloat16)
            sol[2 * x + q, g] = answer
            for d in (1, 2, 3):
                @pl.when(x + d < 4)
                def _(q=q, d=d):
                    sol_send(q, g, d).start()
            pl.when(out_self(q))(lambda q=q: out_keep(q, g).start())
            pl.when(jnp.logical_not(out_self(q)))(lambda q=q: out_send(q, g).start())
            if q == 0:
                @pl.when(g == 0)
                def _():
                    side_wait(2 * x, 1)

                acc[1] += weight * jnp.dot(
                    rows_of[1, 2 * x], expand(answer), preferred_element_type=jnp.float32
                )
        return carry

    lax.fori_loop(0, GROUPS, group, 0)

    @pl.when(late)
    def _():
        for i in range(CHUNKS):
            compute_sigma(i)

    for i in range(CHUNKS):
        for copy in exchange(i):
            copy.wait_send()
        for q in range(2):
            sigma_out(i, q).wait()

        @pl.when(needed)
        def _(i=i):
            hop(i).wait_send()
            for d in (1, 2, 3):
                y_send(0, i, d).wait_send()
            side_own(i).wait_send()

        @pl.when(other_needed)
        def _(i=i):
            for d in (1, 2, 3):
                y_send(1, i, d).wait_send()
            side_send(other_col, i).wait_send()

        for d in (1, 2, 3):
            for half in range(2):
                j = half * 4 + (y + d) % 4

                @pl.when(j < row)
                def _(j=j, i=i):
                    side_send(j, i).wait_send()
    for m in range(2):
        pl.when(jnp.logical_not(right_self(m)))(lambda m=m: right_send(m).wait_send())
    for q in range(2):
        diag_send(q).wait_send()
    for g in range(GROUPS):
        for q in range(2):
            for d in (1, 2, 3):
                @pl.when(x + d < 4)
                def _(q=q, g=g, d=d):
                    sol_send(q, g, d).wait_send()
            pl.when(jnp.logical_not(out_self(q)))(lambda q=q, g=g: out_send(q, g).wait_send())
        for m in range(2):
            from_self = jnp.logical_and(core == zl, zl == m)

            @pl.when(from_self)
            def _(m=m, g=g):
                pltpu.make_async_copy(sol.at[0, g], solved.at[m, g], or_.at[m, g]).wait()

            @pl.when(jnp.logical_not(from_self))
            def _(m=m, g=g):
                remote(sol.at[0, g], solved.at[m, g], os_.at[0, g], or_.at[m, g], sibling).wait_recv()


def on_device(lesser, greater, triples, diag_inverse, right_side):
    count = right_side.shape[0]
    right = right_side.reshape(count, SIDE, 2, GROUPS, LANES).transpose(0, 3, 1, 2, 4)
    right = right.reshape(count, GROUPS, SIDE, 2 * LANES)
    bf16, f32 = jnp.bfloat16, jnp.float32
    dma = pltpu.SemaphoreType.DMA
    hbm = pl.BlockSpec(memory_space=pl.ANY)
    sigma, solved = pl.pallas_call(
        kernel,
        out_shape=(
            jax.ShapeDtypeStruct(lesser.shape, bf16),
            jax.ShapeDtypeStruct(right.shape, bf16),
        ),
        in_specs=[pl.BlockSpec(memory_space=pltpu.SMEM), hbm, hbm, hbm, hbm],
        out_specs=(hbm, hbm),
        scratch_shapes=[pltpu.VMEM((4, 2, PART, SIDE), bf16) for _ in range(CHUNKS)]
        + [pltpu.VMEM((4, 2, SIDE, PART), bf16) for _ in range(CHUNKS)]
        + [
            pltpu.VMEM((4, 2, PART, SIDE), bf16),
            pltpu.VMEM((2, SIDE, WIDE), bf16),
            pltpu.VMEM((2, 8, SIDE, WIDE), bf16),
            pltpu.VMEM((2, SIDE, WIDE), bf16),
            pltpu.VMEM((2, GROUPS, SIDE, 2 * LANES), bf16),
            pltpu.VMEM((2, SIDE, 2 * LANES), f32),
            pltpu.VMEM((8, GROUPS, SIDE, 2 * LANES), bf16),
            dma((CHUNKS, 2)), dma((CHUNKS, 2)), dma((CHUNKS, 2)),
            dma((CHUNKS,)), dma((CHUNKS,)),
            dma((2, CHUNKS, 3)), dma((8, CHUNKS)),
            dma((8, CHUNKS)), dma((8, CHUNKS)),
            dma((2,)), dma((2,)),
            dma((2,)), dma((2,)), dma((2,)),
            dma((2, GROUPS, 3)), dma((8, GROUPS)),
            dma((2, GROUPS)), dma((2, GROUPS)),
            dma((CHUNKS, 2)),
        ],
        compiler_params=pltpu.CompilerParams(
            collective_id=0, has_side_effects=True, vmem_limit_bytes=56 * 1024 * 1024
        ),
        name="second_born",
    )(triples.reshape(-1), lesser, greater, diag_inverse, right)
    solved = solved.reshape(count, GROUPS, SIDE, 2, LANES).transpose(0, 2, 3, 1, 4)
    return (sigma, solved.reshape(right_side.shape))


def solution(mesh):
    placed = (
        P("mom", None, "row", "col"),
        P("mom", None, "col", "row"),
        P(),
        P("mom", None, "row", None),
        P("mom", "row", None, "col"),
    )
    return jax.shard_map(
        on_device,
        mesh=mesh,
        in_specs=placed,
        out_specs=(P("mom", None, "row", "col"), P("mom", "row", None, "col")),
        check_vma=False,
    )
```

```python
import math

import jax
import jax.numpy as jnp
from jax import lax
from jax.experimental import pallas as pl
from jax.experimental.pallas import tpu as pltpu
from jax.sharding import PartitionSpec as P

MESH = pl.DeviceIdType.MESH
SIDE = 384
WIDE = 2 * SIDE
CHUNKS = 3
PART = SIDE // CHUNKS
GROUPS = 3
LANES = 128
PAIRS = 8
SUB = 16


def expand(real, imag):
    tall = jnp.concatenate([real, imag], axis=1)
    turned = jnp.concatenate([-imag, real], axis=1)
    return jnp.concatenate([tall, turned], axis=0)


def kernel(
    triples, lesser, greater, diag, right,
    sigma, solved,
    l0, l1, l2, g0, g1, g2, partner, own_sigma, rows_of, dbuf, rbuf, acc, sol,
    ex_s, ex_r, ps_s, ps_r, loc, zs, zr, ys, yr, ss, sr, rs, rr, dl, ds_, dr, xs, xr, os_, or_, out_s,
):
    lch, gch = (l0, l1, l2), (g0, g1, g2)
    row = lax.axis_index("row")
    col = lax.axis_index("col")
    mom = lax.axis_index("mom")
    x, core = row // 2, row % 2
    zl, y = col // 4, col % 4
    weight = 1.0 / math.sqrt(SIDE * 8)

    def at(x_, core_, y_, zl_):
        return (x_ * 2 + core_, zl_ * 4 + y_, mom)

    pair_dev = (row, col, 1 - mom)
    sibling = at(x, 1 - core, y, zl)
    zflip = at(x, core, y, 1 - zl)

    def y_dev(d):
        return at(x, core, (y + d) % 4, zl)

    def x_dev(d):
        return at(x + d, core, y, zl)

    def remote(src, dst, send, recv, dev):
        return pltpu.make_async_remote_copy(
            src_ref=src, dst_ref=dst, send_sem=send, recv_sem=recv, device_id=dev, device_id_type=MESH
        )

    barrier = pltpu.get_barrier_semaphore()
    peers = [pair_dev, sibling, zflip, at(x, 1 - core, y, 1 - zl), (row, (1 - zl) * 4 + y, 1 - mom)]
    peers += [y_dev(d) for d in (1, 2, 3)]
    peers += [at((x + d) % 4, core, y, zl) for d in (1, 2, 3)]
    for peer in peers:
        pl.semaphore_signal(barrier, inc=1, device_id=peer, device_id_type=MESH)
    pl.semaphore_wait(barrier, len(peers))

    needed = col < row
    last = x == 3
    ring = y < 2 * x + 1
    early = jnp.logical_or(needed, last)
    late = jnp.logical_not(early)
    source = jnp.logical_and(y < row, jnp.logical_not(last))
    split = jnp.logical_and(source, zl == 0)
    relay = jnp.logical_and(source, zl == 1)
    straight = jnp.logical_not(split)
    begin_now = jnp.logical_and(late, jnp.logical_not(ring))
    begin_mid = late & relay & ((x != 2) | (y != 0))
    begin_end = late & ring & jnp.logical_not(begin_mid)
    pass_dev = (row, (1 - zl) * 4 + y, 1 - mom)

    def part(i):
        return pl.ds(i * PART, PART)

    mine = pl.ds(2 * mom, 2)

    def exchange(i):
        return (
            remote(lesser.at[:, :, part(i), :], lch[i].at[mine], ex_s.at[i, 0], ex_r.at[i, 0], pair_dev),
            remote(greater.at[:, :, :, part(i)], gch[i].at[mine], ex_s.at[i, 1], ex_r.at[i, 1], pair_dev),
        )

    def keep(i):
        return (
            pltpu.make_async_copy(lesser.at[:, :, part(i), :], lch[i].at[mine], loc.at[i, 0]),
            pltpu.make_async_copy(greater.at[:, :, :, part(i)], gch[i].at[mine], loc.at[i, 1]),
        )

    def right_self(m):
        return jnp.logical_and(core == zl, zl == m)

    def right_send(m):
        return remote(right.at[m], rbuf.at[core], rs.at[m], rr.at[core], at(x, zl, y, m))

    def right_keep(m):
        return pltpu.make_async_copy(right.at[m], rbuf.at[core], rr.at[core])

    def share_right():
        for m in range(2):
            pl.when(right_self(m))(lambda m=m: right_keep(m).start())
            pl.when(jnp.logical_not(right_self(m)))(lambda m=m: right_send(m).start())

    def start_exchange():
        for i in range(CHUNKS):
            for copy in exchange(i):
                copy.start()

    theirs = pl.ds(2 * (1 - mom), 2)

    def pass_out(i):
        return remote(
            greater.at[:, :, :, part(i)], gch[i].at[theirs], ex_s.at[i, 1], ps_r.at[i], pass_dev
        )

    def pass_on(i):
        return remote(gch[i].at[mine], gch[i].at[theirs], ps_s.at[i], ex_r.at[i, 1], zflip)

    def start_lesser(i):
        exchange(i)[0].start()

    def start_greater(i):
        pl.when(split)(lambda: pass_out(i).start())
        pl.when(straight)(lambda: exchange(i)[1].start())

    pl.when(x == 0)(share_right)

    @pl.when(early)
    def _():
        for i in (0, 1):
            start_lesser(i)
            start_greater(i)
        pl.when(split)(lambda: pass_out(2).start())

    pl.when(begin_now)(start_exchange)

    def diag_keep(q):
        return pltpu.make_async_copy(diag.at[zl, q], dbuf.at[core, :, pl.ds(q * SIDE, SIDE)], dl.at[q])

    def diag_send(q):
        return remote(
            diag.at[zl, q], dbuf.at[core, :, pl.ds(q * SIDE, SIDE)], ds_.at[q], dr.at[q], sibling
        )

    for q in range(2):
        diag_keep(q).start()
        diag_send(q).start()
    for i in range(CHUNKS):
        keep(i)[0].start()
        pl.when(jnp.logical_not(relay))(lambda i=i: keep(i)[1].start())

    def sigma_out(i, q):
        return pltpu.make_async_copy(
            own_sigma.at[:, part(i), pl.ds(q * SIDE, SIDE)], sigma.at[:, q, part(i), :], out_s.at[i, q]
        )

    def compute_sigma(i):
        for copy in exchange(i):
            copy.wait_recv()
        for copy in keep(i):
            copy.wait()

        def turn(k, carry):
            for q in range(2):
                for b in range(3):
                    rows = pl.ds(b * LANES, LANES)
                    partner[k, q, :, rows] = gch[i][k, q, rows, :].T
            return carry

        lax.fori_loop(0, 4, turn, 0)

        def block(s, carry):
            here = pl.ds(pl.multiple_of(s * SUB, SUB), SUB)
            there = pl.ds(pl.multiple_of(i * PART + s * SUB, SUB), SUB)
            for m in range(2):
                sum_real = jnp.zeros((SUB, SIDE), jnp.float32)
                sum_imag = jnp.zeros((SUB, SIDE), jnp.float32)
                for p in range(PAIRS):
                    a, b, c = (triples[n, 2 * mom + m, p] for n in range(3))
                    ar = lch[i][a, 0, here, :].astype(jnp.float32)
                    ai = lch[i][a, 1, here, :].astype(jnp.float32)
                    br = lch[i][b, 0, here, :].astype(jnp.float32)
                    bi = lch[i][b, 1, here, :].astype(jnp.float32)
                    cr = partner[c, 0, here, :].astype(jnp.float32)
                    ci = partner[c, 1, here, :].astype(jnp.float32)
                    pr = ar * br - ai * bi
                    pi = ar * bi + ai * br
                    sum_real += pr * cr - pi * ci
                    sum_imag += pr * ci + pi * cr
                sig_real = (sum_real * (1.0 / PAIRS)).astype(jnp.bfloat16)
                sig_imag = (sum_imag * (1.0 / PAIRS)).astype(jnp.bfloat16)
                own_sigma[m, there, 0:SIDE] = sig_real
                own_sigma[m, there, SIDE:WIDE] = sig_imag

                @pl.when(zl == m)
                def _():
                    rows_of[core, col, there, 0:SIDE] = sig_real
                    rows_of[core, col, there, SIDE:WIDE] = sig_imag
            return carry

        lax.fori_loop(0, PART // SUB, block, 0)
        for q in range(2):
            sigma_out(i, q).start()

    def hop(i):
        return remote(
            own_sigma.at[1 - zl, part(i), :], rows_of.at[core, col, part(i), :], zs.at[i], zr.at[i], zflip
        )

    other_col = (1 - zl) * 4 + y
    other_needed = other_col < row

    def hop_in(i):
        tile = rows_of.at[core, other_col, part(i), :]
        return remote(tile, tile, zs.at[i], zr.at[i], zflip)

    def y_send(t, i, d):
        j = col if t == 0 else other_col
        src = own_sigma.at[zl, part(i), :] if t == 0 else rows_of.at[core, j, part(i), :]
        return remote(src, rows_of.at[core, j, part(i), :], ys.at[t, i, d - 1], yr.at[j, i], y_dev(d))

    def side_send(j, i):
        tile = rows_of.at[core, j, part(i), :]
        return remote(tile, tile, ss.at[j, i], sr.at[j, i], sibling)

    def side_own(i):
        return remote(
            own_sigma.at[zl, part(i), :], rows_of.at[core, col, part(i), :], ss.at[col, i], sr.at[col, i], sibling
        )

    def side_in(j, i):
        tile = rows_of.at[1 - core, j, part(i), :]
        return remote(tile, tile, ss.at[j, i], sr.at[j, i], sibling)

    def gathered(i):
        for d in (1, 2, 3):
            for half in range(2):
                j = half * 4 + (y + d) % 4

                @pl.when(j < row)
                def _(j=j):
                    tile = rows_of.at[core, j, part(i), :]
                    remote(tile, tile, ss.at[j, i], yr.at[j, i], sibling).wait_recv()
                    side_send(j, i).start()

    for q in range(2):
        diag_keep(q).wait()
        dst = dbuf.at[1 - core, :, pl.ds(q * SIDE, SIDE)]
        remote(diag.at[zl, q], dst, ds_.at[q], dr.at[q], sibling).wait_recv()
    def take_right():
        for q in range(2):
            from_self = jnp.logical_and(core == q, zl == core)

            @pl.when(from_self)
            def _(q=q):
                pltpu.make_async_copy(right.at[0], rbuf.at[q], rr.at[q]).wait()

            @pl.when(jnp.logical_not(from_self))
            def _(q=q):
                remote(right.at[0], rbuf.at[q], rs.at[0], rr.at[q], sibling).wait_recv()

    def sol_send(q, g, d):
        tile = sol.at[2 * x + q, g]
        return remote(tile, tile, xs.at[q, g, d - 1], xr.at[2 * x + q, g], x_dev(d))

    def out_self(q):
        return jnp.logical_and(core == q, zl == core)

    def out_tile(m, g):
        start = g * LANES if isinstance(g, int) else pl.multiple_of(g * LANES, LANES)
        return solved.at[m, :, :, pl.ds(start, LANES)]

    def out_send(q, g):
        return remote(
            sol.at[2 * x + q, g], out_tile(zl, g), os_.at[q, g], or_.at[zl, g], at(x, q, y, core)
        )

    def out_keep(q, g):
        return pltpu.make_async_copy(sol.at[2 * x + q, g], out_tile(zl, g), or_.at[zl, g])

    def side_wait(j, which):
        @pl.when(core != which)
        def _():
            for i in range(CHUNKS):
                side_in(j, i).wait_recv()

    def add_right(q, g):
        lanes = pl.ds(pl.multiple_of(g * LANES, LANES), LANES)
        for c in range(2):
            acc[g, q, :, c * LANES : (c + 1) * LANES] += rbuf[q, c, :, lanes].astype(jnp.float32)

    def solve(q, g):
        pending = acc[g, q].astype(jnp.bfloat16)
        answer = jnp.dot(
            dbuf[q], expand(pending[:, :LANES], pending[:, LANES:]), preferred_element_type=jnp.float32
        ).astype(jnp.bfloat16)
        sol[2 * x + q, g, 0] = answer[:, :LANES]
        sol[2 * x + q, g, 1] = answer[:, LANES:]
        pl.when(x < 3)(lambda: sol_send(q, g, 1).start())
        pl.when(x == 0)(lambda: sol_send(q, g, 3).start())
        pl.when(x == 1)(lambda: sol_send(q, g, 2).start())
        pl.when(out_self(q))(lambda: out_keep(q, g).start())
        pl.when(jnp.logical_not(out_self(q)))(lambda: out_send(q, g).start())

    def far_sends(q):
        @pl.when(x == 0)
        def _():
            for g in range(GROUPS):
                sol_send(q, g, 2).start()

    def first(g, carry):
        acc[g] = jnp.zeros(acc.shape[1:], jnp.float32)

        def update(step, c):
            for t in range(2):
                j = 2 * step + t
                tile = sol.at[j, g]
                remote(tile, tile, xs.at[0, g, 0], xr.at[j, g], sibling).wait_recv()

                @pl.when(g == 0)
                def _(j=j):
                    side_wait(j, 0)
                    side_wait(j, 1)

                factor = expand(sol[j, g, 0], sol[j, g, 1])
                for q in range(2):
                    acc[g, q] += weight * jnp.dot(
                        rows_of[q, j], factor, preferred_element_type=jnp.float32
                    )
            return c

        lax.fori_loop(0, x, update, 0)
        pl.when((g == 0) & (x > 0))(take_right)
        for q in range(2):
            add_right(q, g)
        solve(0, g)
        return carry

    def second(g, carry):
        @pl.when(g == 0)
        def _():
            side_wait(2 * x, 1)

        acc[g, 1] += weight * jnp.dot(
            rows_of[1, 2 * x], expand(sol[2 * x, g, 0], sol[2 * x, g, 1]), preferred_element_type=jnp.float32
        )
        solve(1, g)
        return carry

    @pl.when(x == 0)
    def _():
        take_right()
        lax.fori_loop(0, GROUPS, first, 0)
        far_sends(0)

    def relay_step(i):
        @pl.when(relay)
        def _():
            remote(gch[i].at[mine], gch[i].at[mine], ps_s.at[i], ps_r.at[i], zflip).wait_recv()
            pass_on(i).start()

    relay_step(0)
    for i in range(CHUNKS):
        if i + 1 < CHUNKS:
            relay_step(i + 1)
        if i == 1:
            @pl.when(begin_mid)
            def _():
                pl.when(x > 0)(share_right)
                start_exchange()

        @pl.when(early)
        def _(i=i):
            @pl.when(relay)
            def _():
                pass_on(i).wait_send()
                keep(i)[1].start()

            compute_sigma(i)

        @pl.when(needed)
        def _(i=i):
            hop(i).start()
            for d in (1, 3, 2):
                y_send(0, i, d).start()
            side_own(i).start()

        if i == 0:
            pl.when(early)(lambda: start_lesser(2))
        elif i == 1:
            pl.when(early & straight)(lambda: start_greater(2))
        else:
            pl.when((x > 0) & jnp.logical_not(begin_mid))(share_right)

        @pl.when(other_needed)
        def _(i=i):
            hop_in(i).wait_recv()
            for d in (1, 3, 2):
                y_send(1, i, d).start()
            side_send(other_col, i).start()

        if i:
            gathered(i - 1)
    gathered(CHUNKS - 1)
    pl.when(begin_end & (x > 0))(start_exchange)

    def both(g, carry):
        @pl.when(x > 0)
        def _():
            first(g, 0)

        return second(g, carry)

    lax.fori_loop(0, GROUPS, both, 0)
    far_sends(1)
    pl.when(begin_end & (x == 0))(start_exchange)

    @pl.when(late)
    def _():
        @pl.when(relay)
        def _():
            for i in range(CHUNKS):
                pass_on(i).wait_send()
                keep(i)[1].start()

        for i in range(CHUNKS):
            compute_sigma(i)

    for i in range(CHUNKS):
        exchange(i)[0].wait_send()
        pl.when(split)(lambda i=i: pass_out(i).wait_send())
        pl.when(straight)(lambda i=i: exchange(i)[1].wait_send())
        for q in range(2):
            sigma_out(i, q).wait()

        @pl.when(needed)
        def _(i=i):
            hop(i).wait_send()
            for d in (1, 2, 3):
                y_send(0, i, d).wait_send()
            side_own(i).wait_send()

        @pl.when(other_needed)
        def _(i=i):
            for d in (1, 2, 3):
                y_send(1, i, d).wait_send()
            side_send(other_col, i).wait_send()

        for d in (1, 2, 3):
            for half in range(2):
                j = half * 4 + (y + d) % 4

                @pl.when(j < row)
                def _(j=j, i=i):
                    side_send(j, i).wait_send()
    for m in range(2):
        pl.when(jnp.logical_not(right_self(m)))(lambda m=m: right_send(m).wait_send())
    for q in range(2):
        diag_send(q).wait_send()
    for g in range(GROUPS):
        for q in range(2):
            for d in (1, 2, 3):
                @pl.when(x + d < 4)
                def _(q=q, g=g, d=d):
                    sol_send(q, g, d).wait_send()
            pl.when(jnp.logical_not(out_self(q)))(lambda q=q, g=g: out_send(q, g).wait_send())
        for m in range(2):
            from_self = jnp.logical_and(core == zl, zl == m)

            @pl.when(from_self)
            def _(m=m, g=g):
                pltpu.make_async_copy(sol.at[0, g], out_tile(m, g), or_.at[m, g]).wait()

            @pl.when(jnp.logical_not(from_self))
            def _(m=m, g=g):
                remote(sol.at[0, g], out_tile(m, g), os_.at[0, g], or_.at[m, g], sibling).wait_recv()


def on_device(lesser, greater, triples, diag_inverse, right_side):
    right = right_side.transpose(0, 2, 1, 3)
    bf16, f32 = jnp.bfloat16, jnp.float32
    dma = pltpu.SemaphoreType.DMA
    hbm = pl.BlockSpec(memory_space=pl.ANY)
    sigma, solved = pl.pallas_call(
        kernel,
        out_shape=(
            jax.ShapeDtypeStruct(lesser.shape, bf16),
            jax.ShapeDtypeStruct(right.shape, bf16),
        ),
        in_specs=[pl.BlockSpec(memory_space=pltpu.SMEM), hbm, hbm, hbm, hbm],
        out_specs=(hbm, hbm),
        scratch_shapes=[pltpu.VMEM((4, 2, PART, SIDE), bf16) for _ in range(CHUNKS)]
        + [pltpu.VMEM((4, 2, SIDE, PART), bf16) for _ in range(CHUNKS)]
        + [
            pltpu.VMEM((4, 2, PART, SIDE), bf16),
            pltpu.VMEM((2, SIDE, WIDE), bf16),
            pltpu.VMEM((2, 8, SIDE, WIDE), bf16),
            pltpu.VMEM((2, SIDE, WIDE), bf16),
            pltpu.VMEM((2, 2, SIDE, SIDE), bf16),
            pltpu.VMEM((GROUPS, 2, SIDE, 2 * LANES), f32),
            pltpu.VMEM((8, GROUPS, 2, SIDE, LANES), bf16),
            dma((CHUNKS, 2)), dma((CHUNKS, 2)), dma((CHUNKS,)), dma((CHUNKS,)), dma((CHUNKS, 2)),
            dma((CHUNKS,)), dma((CHUNKS,)),
            dma((2, CHUNKS, 3)), dma((8, CHUNKS)),
            dma((8, CHUNKS)), dma((8, CHUNKS)),
            dma((2,)), dma((2,)),
            dma((2,)), dma((2,)), dma((2,)),
            dma((2, GROUPS, 3)), dma((8, GROUPS)),
            dma((2, GROUPS)), dma((2, GROUPS)),
            dma((CHUNKS, 2)),
        ],
        compiler_params=pltpu.CompilerParams(
            collective_id=0, has_side_effects=True, vmem_limit_bytes=56 * 1024 * 1024
        ),
        name="second_born",
    )(triples.transpose(2, 0, 1), lesser, greater, diag_inverse, right)
    return (sigma, solved.transpose(0, 2, 1, 3))


def solution(mesh):
    placed = (
        P("mom", None, "row", "col"),
        P("mom", None, "col", "row"),
        P(),
        P("mom", None, "row", None),
        P("mom", "row", None, "col"),
    )
    return jax.shard_map(
        on_device,
        mesh=mesh,
        in_specs=placed,
        out_specs=(P("mom", None, "row", "col"), P("mom", "row", None, "col")),
        check_vma=False,
    )
```

```python
import math

import jax
import jax.numpy as jnp
from jax import lax
from jax.experimental import pallas as pl
from jax.experimental.pallas import tpu as pltpu
from jax.sharding import PartitionSpec as P

MESH = pl.DeviceIdType.MESH
SIDE = 384
WIDE = 2 * SIDE
CHUNKS = 3
PART = SIDE // CHUNKS
GROUPS = 3
LANES = 128
PAIRS = 8
SUB = 16


def expand(real, imag):
    tall = jnp.concatenate([real, imag], axis=1)
    turned = jnp.concatenate([-imag, real], axis=1)
    return jnp.concatenate([tall, turned], axis=0)


def kernel(
    triples, lesser, greater, diag, right,
    sigma, solved,
    l0, l1, l2, g0, g1, g2, partner, own_sigma, rows_of, dbuf, rbuf, acc, sol, obuf,
    ex_s, ex_r, ps_s, ps_r, loc, zs, zr, ys, yr, ss, sr, rs, rr, dl, ds_, dr, xs, xr, os_, or_, out_s,
):
    lch, gch = (l0, l1, l2), (g0, g1, g2)
    row = lax.axis_index("row")
    col = lax.axis_index("col")
    mom = lax.axis_index("mom")
    x, core = row // 2, row % 2
    zl, y = col // 4, col % 4
    weight = 1.0 / math.sqrt(SIDE * 8)

    def at(x_, core_, y_, zl_):
        return (x_ * 2 + core_, zl_ * 4 + y_, mom)

    pair_dev = (row, col, 1 - mom)
    sibling = at(x, 1 - core, y, zl)
    zflip = at(x, core, y, 1 - zl)

    def y_dev(d):
        return at(x, core, (y + d) % 4, zl)

    def x_dev(d):
        return at(x + d, core, y, zl)

    def remote(src, dst, send, recv, dev):
        return pltpu.make_async_remote_copy(
            src_ref=src, dst_ref=dst, send_sem=send, recv_sem=recv, device_id=dev, device_id_type=MESH
        )

    barrier = pltpu.get_barrier_semaphore()
    peers = [pair_dev, sibling, zflip, at(x, 1 - core, y, 1 - zl), (row, (1 - zl) * 4 + y, 1 - mom)]
    peers += [y_dev(d) for d in (1, 2, 3)]
    peers += [at((x + d) % 4, core, y, zl) for d in (1, 2, 3)]
    for peer in peers:
        pl.semaphore_signal(barrier, inc=1, device_id=peer, device_id_type=MESH)
    pl.semaphore_wait(barrier, len(peers))

    needed = col < row
    last = x == 3
    ring = y < 2 * x + 1
    early = jnp.logical_or(needed, last)
    late = jnp.logical_not(early)
    source = (y < row) & jnp.logical_not(last) & ((row != 5) | (y != 0))
    split = jnp.logical_and(source, zl == 0)
    relay = jnp.logical_and(source, zl == 1)
    straight = jnp.logical_not(split)
    begin_now = jnp.logical_and(late, jnp.logical_not(ring))
    begin_mid = late & relay & ((x != 2) | (y != 0))
    begin_end = late & ring & jnp.logical_not(begin_mid)
    pass_dev = (row, (1 - zl) * 4 + y, 1 - mom)

    def part(i):
        return pl.ds(i * PART, PART)

    mine = pl.ds(2 * mom, 2)

    def exchange(i):
        return (
            remote(lesser.at[:, :, part(i), :], lch[i].at[mine], ex_s.at[i, 0], ex_r.at[i, 0], pair_dev),
            remote(greater.at[:, :, :, part(i)], gch[i].at[mine], ex_s.at[i, 1], ex_r.at[i, 1], pair_dev),
        )

    def keep(i):
        return (
            pltpu.make_async_copy(lesser.at[:, :, part(i), :], lch[i].at[mine], loc.at[i, 0]),
            pltpu.make_async_copy(greater.at[:, :, :, part(i)], gch[i].at[mine], loc.at[i, 1]),
        )

    def right_self(m):
        return jnp.logical_and(core == zl, zl == m)

    def right_send(m):
        return remote(right.at[m], rbuf.at[core], rs.at[m], rr.at[core], at(x, zl, y, m))

    def right_keep(m):
        return pltpu.make_async_copy(right.at[m], rbuf.at[core], rr.at[core])

    def share_right():
        for m in range(2):
            pl.when(right_self(m))(lambda m=m: right_keep(m).start())
            pl.when(jnp.logical_not(right_self(m)))(lambda m=m: right_send(m).start())

    def start_exchange():
        for i in range(CHUNKS):
            for copy in exchange(i):
                copy.start()

    theirs = pl.ds(2 * (1 - mom), 2)

    def pass_out(i):
        return remote(
            greater.at[:, :, :, part(i)], gch[i].at[theirs], ex_s.at[i, 1], ps_r.at[i], pass_dev
        )

    def pass_on(i):
        return remote(gch[i].at[mine], gch[i].at[theirs], ps_s.at[i], ex_r.at[i, 1], zflip)

    def start_lesser(i):
        exchange(i)[0].start()

    def start_greater(i):
        pl.when(split)(lambda: pass_out(i).start())
        pl.when(straight)(lambda: exchange(i)[1].start())

    @pl.when(early)
    def _():
        for i in (0, 1):
            start_lesser(i)
            start_greater(i)
        pl.when(split)(lambda: pass_out(2).start())
        pl.when(x == 0)(lambda: start_lesser(2))

    pl.when(x == 0)(share_right)
    pl.when(begin_now)(start_exchange)

    def diag_keep(q):
        return pltpu.make_async_copy(diag.at[zl, q], dbuf.at[core, :, pl.ds(q * SIDE, SIDE)], dl.at[q])

    def diag_send(q):
        return remote(
            diag.at[zl, q], dbuf.at[core, :, pl.ds(q * SIDE, SIDE)], ds_.at[q], dr.at[q], sibling
        )

    for q in range(2):
        diag_keep(q).start()
        diag_send(q).start()
    for i in range(CHUNKS):
        keep(i)[0].start()
        pl.when(jnp.logical_not(relay))(lambda i=i: keep(i)[1].start())

    def sigma_out(i, q):
        return pltpu.make_async_copy(
            own_sigma.at[:, part(i), pl.ds(q * SIDE, SIDE)], sigma.at[:, q, part(i), :], out_s.at[i, q]
        )

    def compute_sigma(i):
        for copy in exchange(i):
            copy.wait_recv()
        for copy in keep(i):
            copy.wait()

        def turn(k, carry):
            for q in range(2):
                for b in range(3):
                    rows = pl.ds(b * LANES, LANES)
                    partner[k, q, :, rows] = gch[i][k, q, rows, :].T
            return carry

        lax.fori_loop(0, 4, turn, 0)

        def block(s, carry):
            here = pl.ds(pl.multiple_of(s * SUB, SUB), SUB)
            there = pl.ds(pl.multiple_of(i * PART + s * SUB, SUB), SUB)
            for m in range(2):
                sum_real = jnp.zeros((SUB, SIDE), jnp.float32)
                sum_imag = jnp.zeros((SUB, SIDE), jnp.float32)
                for p in range(PAIRS):
                    a, b, c = (triples[n, 2 * mom + m, p] for n in range(3))
                    ar = lch[i][a, 0, here, :].astype(jnp.float32)
                    ai = lch[i][a, 1, here, :].astype(jnp.float32)
                    br = lch[i][b, 0, here, :].astype(jnp.float32)
                    bi = lch[i][b, 1, here, :].astype(jnp.float32)
                    cr = partner[c, 0, here, :].astype(jnp.float32)
                    ci = partner[c, 1, here, :].astype(jnp.float32)
                    pr = ar * br - ai * bi
                    pi = ar * bi + ai * br
                    sum_real += pr * cr - pi * ci
                    sum_imag += pr * ci + pi * cr
                sig_real = (sum_real * (1.0 / PAIRS)).astype(jnp.bfloat16)
                sig_imag = (sum_imag * (1.0 / PAIRS)).astype(jnp.bfloat16)
                own_sigma[m, there, 0:SIDE] = sig_real
                own_sigma[m, there, SIDE:WIDE] = sig_imag

                @pl.when(zl == m)
                def _():
                    rows_of[core, col, there, 0:SIDE] = sig_real
                    rows_of[core, col, there, SIDE:WIDE] = sig_imag
            return carry

        lax.fori_loop(0, PART // SUB, block, 0)
        for q in range(2):
            sigma_out(i, q).start()

    def hop(i):
        return remote(
            own_sigma.at[1 - zl, part(i), :], rows_of.at[core, col, part(i), :], zs.at[i], zr.at[i], zflip
        )

    other_col = (1 - zl) * 4 + y
    other_needed = other_col < row

    def hop_in(i):
        tile = rows_of.at[core, other_col, part(i), :]
        return remote(tile, tile, zs.at[i], zr.at[i], zflip)

    def y_send(t, i, d):
        j = col if t == 0 else other_col
        src = own_sigma.at[zl, part(i), :] if t == 0 else rows_of.at[core, j, part(i), :]
        return remote(src, rows_of.at[core, j, part(i), :], ys.at[t, i, d - 1], yr.at[j, i], y_dev(d))

    def side_send(j, i):
        tile = rows_of.at[core, j, part(i), :]
        return remote(tile, tile, ss.at[j, i], sr.at[j, i], sibling)

    def side_own(i):
        return remote(
            own_sigma.at[zl, part(i), :], rows_of.at[core, col, part(i), :], ss.at[col, i], sr.at[col, i], sibling
        )

    def side_in(j, i):
        tile = rows_of.at[1 - core, j, part(i), :]
        return remote(tile, tile, ss.at[j, i], sr.at[j, i], sibling)

    def gathered(i):
        for d in (1, 2, 3):
            for half in range(2):
                j = half * 4 + (y + d) % 4

                @pl.when(j < row)
                def _(j=j):
                    tile = rows_of.at[core, j, part(i), :]
                    remote(tile, tile, ss.at[j, i], yr.at[j, i], sibling).wait_recv()
                    side_send(j, i).start()

    for q in range(2):
        diag_keep(q).wait()
        dst = dbuf.at[1 - core, :, pl.ds(q * SIDE, SIDE)]
        remote(diag.at[zl, q], dst, ds_.at[q], dr.at[q], sibling).wait_recv()
    def take_right():
        for q in range(2):
            from_self = jnp.logical_and(core == q, zl == core)

            @pl.when(from_self)
            def _(q=q):
                pltpu.make_async_copy(right.at[0], rbuf.at[q], rr.at[q]).wait()

            @pl.when(jnp.logical_not(from_self))
            def _(q=q):
                remote(right.at[0], rbuf.at[q], rs.at[0], rr.at[q], sibling).wait_recv()

    def sol_send(q, g, d):
        tile = sol.at[2 * x + q, g]
        return remote(tile, tile, xs.at[q, g, d - 1], xr.at[2 * x + q, g], x_dev(d))

    def out_self(q):
        return jnp.logical_and(core == q, zl == core)

    def out_tile(m, g):
        start = g * LANES if isinstance(g, int) else pl.multiple_of(g * LANES, LANES)
        return solved.at[m, :, :, pl.ds(start, LANES)]

    def out_send(q, g):
        return remote(
            obuf.at[q, g], out_tile(zl, g), os_.at[q, g], or_.at[zl, g], at(x, q, y, core)
        )

    def out_keep(q, g):
        return pltpu.make_async_copy(obuf.at[q, g], out_tile(zl, g), or_.at[zl, g])

    def side_wait(j, which):
        @pl.when(core != which)
        def _():
            for i in range(CHUNKS):
                side_in(j, i).wait_recv()

    def add_right(q, g):
        lanes = pl.ds(pl.multiple_of(g * LANES, LANES), LANES)
        for c in range(2):
            acc[g, q, :, c * LANES : (c + 1) * LANES] += rbuf[q, :, c, lanes].astype(jnp.float32)

    def solve(q, g):
        pending = acc[g, q].astype(jnp.bfloat16)
        answer = jnp.dot(
            dbuf[q], expand(pending[:, :LANES], pending[:, LANES:]), preferred_element_type=jnp.float32
        ).astype(jnp.bfloat16)
        real, imag = answer[:, :LANES], answer[:, LANES:]
        sol[2 * x + q, g, 0] = real
        sol[2 * x + q, g, 1] = imag
        pl.when(x < 3)(lambda: sol_send(q, g, 1).start())
        pl.when(x == 0)(lambda: sol_send(q, g, 3).start())
        obuf[q, g] = jnp.stack([real, imag], axis=1)
        pl.when(out_self(q))(lambda: out_keep(q, g).start())
        pl.when(jnp.logical_not(out_self(q)))(lambda: out_send(q, g).start())

    def row_on(j, g):
        tile = sol.at[j, g]
        return remote(tile, tile, xs.at[j, g, 0], xr.at[j, g], x_dev(-1))

    def relay_row(j):
        @pl.when(last)
        def _():
            for g in range(GROUPS):
                row_on(j, g).wait_recv()
                row_on(j, g).start()

    def first(g, carry):
        acc[g] = jnp.zeros(acc.shape[1:], jnp.float32)

        def update(step, c):
            for t in range(2):
                j = 2 * step + t
                tile = sol.at[j, g]

                @pl.when(jnp.logical_not(last) | (j > 1))
                def _(tile=tile, j=j):
                    remote(tile, tile, xs.at[0, g, 0], xr.at[j, g], sibling).wait_recv()

                @pl.when(g == 0)
                def _(j=j):
                    side_wait(j, 0)
                    side_wait(j, 1)

                factor = expand(sol[j, g, 0], sol[j, g, 1])
                for q in range(2):
                    acc[g, q] += weight * jnp.dot(
                        rows_of[q, j], factor, preferred_element_type=jnp.float32
                    )
            return c

        lax.fori_loop(0, x, update, 0)
        pl.when((g == 0) & (x > 0))(take_right)
        for q in range(2):
            add_right(q, g)
        solve(0, g)
        return carry

    def second(g, carry):
        @pl.when(g == 0)
        def _():
            side_wait(2 * x, 1)

        acc[g, 1] += weight * jnp.dot(
            rows_of[1, 2 * x], expand(sol[2 * x, g, 0], sol[2 * x, g, 1]), preferred_element_type=jnp.float32
        )
        solve(1, g)
        return carry

    @pl.when(x == 0)
    def _():
        take_right()
        lax.fori_loop(0, GROUPS, first, 0)

    def relay_step(i):
        @pl.when(relay)
        def _():
            remote(gch[i].at[mine], gch[i].at[mine], ps_s.at[i], ps_r.at[i], zflip).wait_recv()
            pass_on(i).start()

    relay_step(0)
    for i in range(CHUNKS):
        if i + 1 < CHUNKS:
            relay_step(i + 1)
        if i:
            relay_row(i - 1)
        if i == 1:
            @pl.when(begin_mid)
            def _():
                pl.when(x > 0)(share_right)
                start_exchange()

        @pl.when(early)
        def _(i=i):
            @pl.when(relay)
            def _():
                pass_on(i).wait_send()
                keep(i)[1].start()

            compute_sigma(i)

        @pl.when(needed)
        def _(i=i):
            hop(i).start()
            for d in (1, 3, 2):
                y_send(0, i, d).start()
            side_own(i).start()

        if i == 0:
            pl.when(early & (x > 0))(lambda: start_lesser(2))
        elif i == 1:
            pl.when(early & straight)(lambda: start_greater(2))
        else:
            pl.when((x > 0) & jnp.logical_not(begin_mid))(share_right)

        @pl.when(other_needed)
        def _(i=i):
            hop_in(i).wait_recv()
            for d in (1, 3, 2):
                y_send(1, i, d).start()
            side_send(other_col, i).start()

        if i:
            gathered(i - 1)
    gathered(CHUNKS - 1)
    pl.when(begin_end & (x > 0))(start_exchange)

    def both(g, carry):
        @pl.when(x > 0)
        def _():
            first(g, 0)

        return second(g, carry)

    lax.fori_loop(0, GROUPS, both, 0)

    @pl.when(x == 1)
    def _():
        for g in range(GROUPS):
            for q in range(2):
                sol_send(q, g, 2).start()

    pl.when(begin_end & (x == 0))(start_exchange)

    @pl.when(late)
    def _():
        @pl.when(relay)
        def _():
            for i in range(CHUNKS):
                pass_on(i).wait_send()
                keep(i)[1].start()

        for i in range(CHUNKS):
            compute_sigma(i)

    for i in range(CHUNKS):
        exchange(i)[0].wait_send()
        pl.when(split)(lambda i=i: pass_out(i).wait_send())
        pl.when(straight)(lambda i=i: exchange(i)[1].wait_send())
        for q in range(2):
            sigma_out(i, q).wait()

        @pl.when(needed)
        def _(i=i):
            hop(i).wait_send()
            for d in (1, 2, 3):
                y_send(0, i, d).wait_send()
            side_own(i).wait_send()

        @pl.when(other_needed)
        def _(i=i):
            for d in (1, 2, 3):
                y_send(1, i, d).wait_send()
            side_send(other_col, i).wait_send()

        for d in (1, 2, 3):
            for half in range(2):
                j = half * 4 + (y + d) % 4

                @pl.when(j < row)
                def _(j=j, i=i):
                    side_send(j, i).wait_send()
    for m in range(2):
        pl.when(jnp.logical_not(right_self(m)))(lambda m=m: right_send(m).wait_send())
    for q in range(2):
        diag_send(q).wait_send()
    for g in range(GROUPS):
        for q in range(2):
            pl.when(x < 3)(lambda q=q, g=g: sol_send(q, g, 1).wait_send())
            pl.when(x == 1)(lambda q=q, g=g: sol_send(q, g, 2).wait_send())
            pl.when(x == 0)(lambda q=q, g=g: sol_send(q, g, 3).wait_send())
            pl.when(last)(lambda q=q, g=g: row_on(q, g).wait_send())
            pl.when(jnp.logical_not(out_self(q)))(lambda q=q, g=g: out_send(q, g).wait_send())
        for m in range(2):
            from_self = jnp.logical_and(core == zl, zl == m)

            @pl.when(from_self)
            def _(m=m, g=g):
                pltpu.make_async_copy(obuf.at[0, g], out_tile(m, g), or_.at[m, g]).wait()

            @pl.when(jnp.logical_not(from_self))
            def _(m=m, g=g):
                remote(obuf.at[0, g], out_tile(m, g), os_.at[0, g], or_.at[m, g], sibling).wait_recv()


def on_device(lesser, greater, triples, diag_inverse, right_side):
    bf16, f32 = jnp.bfloat16, jnp.float32
    dma = pltpu.SemaphoreType.DMA
    hbm = pl.BlockSpec(memory_space=pl.ANY)
    sigma, solved = pl.pallas_call(
        kernel,
        out_shape=(
            jax.ShapeDtypeStruct(lesser.shape, bf16),
            jax.ShapeDtypeStruct(right_side.shape, bf16),
        ),
        in_specs=[pl.BlockSpec(memory_space=pltpu.SMEM), hbm, hbm, hbm, hbm],
        out_specs=(hbm, hbm),
        scratch_shapes=[pltpu.VMEM((4, 2, PART, SIDE), bf16) for _ in range(CHUNKS)]
        + [pltpu.VMEM((4, 2, SIDE, PART), bf16) for _ in range(CHUNKS)]
        + [
            pltpu.VMEM((4, 2, PART, SIDE), bf16),
            pltpu.VMEM((2, SIDE, WIDE), bf16),
            pltpu.VMEM((2, 8, SIDE, WIDE), bf16),
            pltpu.VMEM((2, SIDE, WIDE), bf16),
            pltpu.VMEM((2, SIDE, 2, SIDE), bf16),
            pltpu.VMEM((GROUPS, 2, SIDE, 2 * LANES), f32),
            pltpu.VMEM((8, GROUPS, 2, SIDE, LANES), bf16),
            pltpu.VMEM((2, GROUPS, SIDE, 2, LANES), bf16),
            dma((CHUNKS, 2)), dma((CHUNKS, 2)), dma((CHUNKS,)), dma((CHUNKS,)), dma((CHUNKS, 2)),
            dma((CHUNKS,)), dma((CHUNKS,)),
            dma((2, CHUNKS, 3)), dma((8, CHUNKS)),
            dma((8, CHUNKS)), dma((8, CHUNKS)),
            dma((2,)), dma((2,)),
            dma((2,)), dma((2,)), dma((2,)),
            dma((2, GROUPS, 3)), dma((8, GROUPS)),
            dma((2, GROUPS)), dma((2, GROUPS)),
            dma((CHUNKS, 2)),
        ],
        compiler_params=pltpu.CompilerParams(
            collective_id=0, has_side_effects=True, vmem_limit_bytes=56 * 1024 * 1024
        ),
        name="second_born",
    )(triples.transpose(2, 0, 1), lesser, greater, diag_inverse, right_side)
    return (sigma, solved)


def solution(mesh):
    placed = (
        P("mom", None, "row", "col"),
        P("mom", None, "col", "row"),
        P(),
        P("mom", None, "row", None),
        P("mom", "row", None, "col"),
    )
    return jax.shard_map(
        on_device,
        mesh=mesh,
        in_specs=placed,
        out_specs=(P("mom", None, "row", "col"), P("mom", "row", None, "col")),
        check_vma=False,
    )
```

```python
import math

import jax
import jax.numpy as jnp
from jax import lax
from jax.experimental import pallas as pl
from jax.experimental.pallas import tpu as pltpu
from jax.sharding import PartitionSpec as P

MESH = pl.DeviceIdType.MESH
SIDE = 384
WIDE = 2 * SIDE
CHUNKS = 3
PART = SIDE // CHUNKS
GROUPS = 3
LANES = 128
PAIRS = 8
SUB = 16


def expand(real, imag):
    tall = jnp.concatenate([real, imag], axis=1)
    turned = jnp.concatenate([-imag, real], axis=1)
    return jnp.concatenate([tall, turned], axis=0)


def kernel(
    triples, lesser, greater, diag, right,
    sigma, solved,
    l0, l1, l2, g0, g1, g2, partner, own_sigma, rows_of, dbuf, rbuf, acc, sol, obuf, raw, plan,
    ex_s, ex_r, ps_s, ps_r, loc, zs, zr, ys, yr, ss, sr, rs, rr, dl, ds_, dr, xs, xr, os_, or_, out_s, raw_s,
):
    lch, gch = (l0, l1, l2), (g0, g1, g2)
    row = lax.axis_index("row")
    col = lax.axis_index("col")
    mom = lax.axis_index("mom")
    x, core = row // 2, row % 2
    zl, y = col // 4, col % 4
    weight = 1.0 / math.sqrt(SIDE * 8)

    def at(x_, core_, y_, zl_):
        return (x_ * 2 + core_, zl_ * 4 + y_, mom)

    pair_dev = (row, col, 1 - mom)
    sibling = at(x, 1 - core, y, zl)
    zflip = at(x, core, y, 1 - zl)

    def y_dev(d):
        return at(x, core, (y + d) % 4, zl)

    def x_dev(d):
        return at(x + d, core, y, zl)

    def remote(src, dst, send, recv, dev):
        return pltpu.make_async_remote_copy(
            src_ref=src, dst_ref=dst, send_sem=send, recv_sem=recv, device_id=dev, device_id_type=MESH
        )

    barrier = pltpu.get_barrier_semaphore()
    peers = [pair_dev, sibling, zflip, at(x, 1 - core, y, 1 - zl), (row, (1 - zl) * 4 + y, 1 - mom)]
    peers += [y_dev(d) for d in (1, 2, 3)]
    peers += [at((x + d) % 4, core, y, zl) for d in (1, 2, 3)]
    for peer in peers:
        pl.semaphore_signal(barrier, inc=1, device_id=peer, device_id_type=MESH)
    pl.semaphore_wait(barrier, len(peers))

    needed = col < row
    last = x == 3
    ring = y < 2 * x + 1
    early = jnp.logical_or(needed, last)
    late = jnp.logical_not(early)
    source = (y < row) & jnp.logical_not(last) & ((row != 5) | (y != 0))
    split = jnp.logical_and(source, zl == 0)
    relay = jnp.logical_and(source, zl == 1)
    straight = jnp.logical_not(split)
    begin_now = jnp.logical_and(late, jnp.logical_not(ring))
    begin_mid = late & relay & ((x != 2) | (y != 0))
    begin_end = late & ring & jnp.logical_not(begin_mid)
    three = ((x == 2) & (y == 0)) | ((x == 1) & (core == 0))
    pass_dev = (row, (1 - zl) * 4 + y, 1 - mom)

    def part(i):
        return pl.ds(i * PART, PART)

    mine = pl.ds(2 * mom, 2)

    def exchange(i):
        return (
            remote(lesser.at[:, :, part(i), :], lch[i].at[mine], ex_s.at[i, 0], ex_r.at[i, 0], pair_dev),
            remote(greater.at[:, :, :, part(i)], gch[i].at[mine], ex_s.at[i, 1], ex_r.at[i, 1], pair_dev),
        )

    def keep(i):
        return (
            pltpu.make_async_copy(lesser.at[:, :, part(i), :], lch[i].at[mine], loc.at[i, 0]),
            pltpu.make_async_copy(greater.at[:, :, :, part(i)], gch[i].at[mine], loc.at[i, 1]),
        )

    def right_self(m):
        return jnp.logical_and(core == zl, zl == m)

    def right_send(m, g):
        return remote(plan.at[m, g], rbuf.at[core, g], rs.at[m, g], rr.at[core, g], at(x, zl, y, m))

    def right_keep(m, g):
        return pltpu.make_async_copy(plan.at[m, g], rbuf.at[core, g], rr.at[core, g])

    def share_right():
        for g in range(GROUPS):
            for m in range(2):
                pl.when(right_self(m))(lambda m=m: right_keep(m, g).start())
                pl.when(jnp.logical_not(right_self(m)))(lambda m=m: right_send(m, g).start())

    raw_in = pltpu.make_async_copy(right, raw, raw_s.at[0])
    raw_in.start()

    def turn_right():
        raw_in.wait()

        def turn_group(t, carry):
            m, g = t // GROUPS, t % GROUPS
            lanes = pl.ds(pl.multiple_of(g * LANES, LANES), LANES)
            both_parts = raw[m, :, :, lanes].astype(jnp.float32)
            for c in range(2):
                plan[m, g, :, c * LANES : (c + 1) * LANES] = both_parts[:, c, :].astype(jnp.bfloat16)
            return carry

        lax.fori_loop(0, 2 * GROUPS, turn_group, 0)

    def start_exchange():
        for i in range(CHUNKS):
            for copy in exchange(i):
                copy.start()

    theirs = pl.ds(2 * (1 - mom), 2)

    def pass_out(i):
        return remote(
            greater.at[:, :, :, part(i)], gch[i].at[theirs], ex_s.at[i, 1], ps_r.at[i], pass_dev
        )

    def pass_on(i):
        return remote(gch[i].at[mine], gch[i].at[theirs], ps_s.at[i], ex_r.at[i, 1], zflip)

    def start_lesser(i):
        exchange(i)[0].start()

    RELAYED = 2

    def start_greater(i):
        if i < RELAYED:
            pl.when(split)(lambda: pass_out(i).start())
            pl.when(straight)(lambda: exchange(i)[1].start())
        else:
            pl.when(jnp.logical_not(split & three))(lambda: exchange(i)[1].start())

    @pl.when(early)
    def _():
        for i in (0, 1):
            start_lesser(i)
            start_greater(i)

        pl.when(split & three)(lambda: pass_out(2).start())

        @pl.when(x == 0)
        def _():
            start_lesser(2)
            start_greater(2)

    turn_right()
    pl.when(x == 0)(share_right)
    pl.when(begin_now)(start_exchange)

    def diag_keep(q):
        return pltpu.make_async_copy(diag.at[zl, q], dbuf.at[core, :, pl.ds(q * SIDE, SIDE)], dl.at[q])

    def diag_send(q):
        return remote(
            diag.at[zl, q], dbuf.at[core, :, pl.ds(q * SIDE, SIDE)], ds_.at[q], dr.at[q], sibling
        )

    for q in range(2):
        diag_keep(q).start()
        diag_send(q).start()
    for i in range(CHUNKS):
        keep(i)[0].start()
        if i < RELAYED:
            pl.when(jnp.logical_not(relay))(lambda i=i: keep(i)[1].start())
        else:
            pl.when(jnp.logical_not(relay & three))(lambda i=i: keep(i)[1].start())

    def sigma_out(i, q):
        return pltpu.make_async_copy(
            own_sigma.at[:, part(i), pl.ds(q * SIDE, SIDE)], sigma.at[:, q, part(i), :], out_s.at[i, q]
        )

    def compute_sigma(i):
        for copy in exchange(i):
            copy.wait_recv()
        for copy in keep(i):
            copy.wait()

        def turn(k, carry):
            for q in range(2):
                for b in range(3):
                    rows = pl.ds(b * LANES, LANES)
                    partner[k, q, :, rows] = gch[i][k, q, rows, :].T
            return carry

        lax.fori_loop(0, 4, turn, 0)

        def block(m, s, carry):
            here = pl.ds(pl.multiple_of(s * SUB, SUB), SUB)
            there = pl.ds(pl.multiple_of(i * PART + s * SUB, SUB), SUB)
            sum_real = jnp.zeros((SUB, SIDE), jnp.float32)
            sum_imag = jnp.zeros((SUB, SIDE), jnp.float32)
            for p in range(PAIRS):
                a, b, c = (triples[n, 2 * mom + m, p] for n in range(3))
                ar = lch[i][a, 0, here, :].astype(jnp.float32)
                ai = lch[i][a, 1, here, :].astype(jnp.float32)
                br = lch[i][b, 0, here, :].astype(jnp.float32)
                bi = lch[i][b, 1, here, :].astype(jnp.float32)
                cr = partner[c, 0, here, :].astype(jnp.float32)
                ci = partner[c, 1, here, :].astype(jnp.float32)
                pr = ar * br - ai * bi
                pi = ar * bi + ai * br
                sum_real += pr * cr - pi * ci
                sum_imag += pr * ci + pi * cr
            sig_real = (sum_real * (1.0 / PAIRS)).astype(jnp.bfloat16)
            sig_imag = (sum_imag * (1.0 / PAIRS)).astype(jnp.bfloat16)
            own_sigma[m, there, 0:SIDE] = sig_real
            own_sigma[m, there, SIDE:WIDE] = sig_imag

            @pl.when(zl == m)
            def _():
                rows_of[core, col, there, 0:SIDE] = sig_real
                rows_of[core, col, there, SIDE:WIDE] = sig_imag
            return carry

        lax.fori_loop(0, PART // SUB, lambda s, c: block(1 - zl, s, c), 0)
        pl.when(needed)(lambda: hop(i).start())
        lax.fori_loop(0, PART // SUB, lambda s, c: block(zl, s, c), 0)
        for q in range(2):
            sigma_out(i, q).start()

    def hop(i):
        return remote(
            own_sigma.at[1 - zl, part(i), :], rows_of.at[core, col, part(i), :], zs.at[i], zr.at[i], zflip
        )

    other_col = (1 - zl) * 4 + y
    other_needed = other_col < row

    def hop_in(i):
        tile = rows_of.at[core, other_col, part(i), :]
        return remote(tile, tile, zs.at[i], zr.at[i], zflip)

    def y_send(t, i, d):
        j = col if t == 0 else other_col
        src = own_sigma.at[zl, part(i), :] if t == 0 else rows_of.at[core, j, part(i), :]
        return remote(src, rows_of.at[core, j, part(i), :], ys.at[t, i, d - 1], yr.at[j, i], y_dev(d))

    def side_send(j, i):
        tile = rows_of.at[core, j, part(i), :]
        return remote(tile, tile, ss.at[j, i], sr.at[j, i], sibling)

    def side_own(i):
        return remote(
            own_sigma.at[zl, part(i), :], rows_of.at[core, col, part(i), :], ss.at[col, i], sr.at[col, i], sibling
        )

    def side_in(j, i):
        tile = rows_of.at[1 - core, j, part(i), :]
        return remote(tile, tile, ss.at[j, i], sr.at[j, i], sibling)

    def gathered(i):
        for d in (1, 2, 3):
            for half in range(2):
                j = half * 4 + (y + d) % 4

                @pl.when(j < row)
                def _(j=j):
                    tile = rows_of.at[core, j, part(i), :]
                    remote(tile, tile, ss.at[j, i], yr.at[j, i], sibling).wait_recv()
                    side_send(j, i).start()

    for q in range(2):
        diag_keep(q).wait()
        dst = dbuf.at[1 - core, :, pl.ds(q * SIDE, SIDE)]
        remote(diag.at[zl, q], dst, ds_.at[q], dr.at[q], sibling).wait_recv()
    def take_right(g):
        for q in range(2):
            from_self = jnp.logical_and(core == q, zl == core)

            @pl.when(from_self)
            def _(q=q):
                pltpu.make_async_copy(plan.at[0, g], rbuf.at[q, g], rr.at[q, g]).wait()

            @pl.when(jnp.logical_not(from_self))
            def _(q=q):
                remote(plan.at[0, g], rbuf.at[q, g], rs.at[0, g], rr.at[q, g], sibling).wait_recv()

    def sol_send(q, g, d):
        tile = sol.at[2 * x + q, g]
        return remote(tile, tile, xs.at[q, g, d - 1], xr.at[2 * x + q, g], x_dev(d))

    def out_self(q):
        return jnp.logical_and(core == q, zl == core)

    def out_tile(m, g):
        start = g * LANES if isinstance(g, int) else pl.multiple_of(g * LANES, LANES)
        return solved.at[m, :, :, pl.ds(start, LANES)]

    def out_send(q, g):
        return remote(
            obuf.at[q, g], out_tile(zl, g), os_.at[q, g], or_.at[zl, g], at(x, q, y, core)
        )

    def out_keep(q, g):
        return pltpu.make_async_copy(obuf.at[q, g], out_tile(zl, g), or_.at[zl, g])

    def side_wait(j, which):
        @pl.when(core != which)
        def _():
            for i in range(CHUNKS):
                side_in(j, i).wait_recv()

    def add_right(q, g):
        acc[g, q] += rbuf[q, g].astype(jnp.float32)

    def solve(q, g):
        pending = acc[g, q].astype(jnp.bfloat16)
        answer = jnp.dot(
            dbuf[q], expand(pending[:, :LANES], pending[:, LANES:]), preferred_element_type=jnp.float32
        ).astype(jnp.bfloat16)
        real, imag = answer[:, :LANES], answer[:, LANES:]
        sol[2 * x + q, g, 0] = real
        sol[2 * x + q, g, 1] = imag
        pl.when(x < 3)(lambda: sol_send(q, g, 1).start())
        pl.when(x == 0)(lambda: sol_send(q, g, 3).start())
        obuf[q, g] = jnp.stack([real, imag], axis=1)
        pl.when(out_self(q))(lambda: out_keep(q, g).start())
        pl.when(jnp.logical_not(out_self(q)))(lambda: out_send(q, g).start())

    def row_on(j, g):
        tile = sol.at[j, g]
        return remote(tile, tile, xs.at[j, g, 0], xr.at[j, g], x_dev(-1))

    def relay_row(j, groups):
        @pl.when(last)
        def _():
            for g in groups:
                row_on(j, g).wait_recv()
                row_on(j, g).start()

    def first(g, carry):
        acc[g] = jnp.zeros(acc.shape[1:], jnp.float32)

        def update(step, c):
            for t in range(2):
                j = 2 * step + t
                tile = sol.at[j, g]

                @pl.when(jnp.logical_not(last) | (j > 1))
                def _(tile=tile, j=j):
                    remote(tile, tile, xs.at[0, g, 0], xr.at[j, g], sibling).wait_recv()

                @pl.when(g == 0)
                def _(j=j):
                    side_wait(j, 0)
                    side_wait(j, 1)

                factor = expand(sol[j, g, 0], sol[j, g, 1])
                for q in range(2):
                    acc[g, q] += weight * jnp.dot(
                        rows_of[q, j], factor, preferred_element_type=jnp.float32
                    )
            return c

        lax.fori_loop(0, x, update, 0)
        take_right(g)
        for q in range(2):
            add_right(q, g)
        solve(0, g)
        return carry

    def second(g, carry):
        @pl.when(g == 0)
        def _():
            side_wait(2 * x, 1)

        acc[g, 1] += weight * jnp.dot(
            rows_of[1, 2 * x], expand(sol[2 * x, g, 0], sol[2 * x, g, 1]), preferred_element_type=jnp.float32
        )
        solve(1, g)
        return carry

    @pl.when(x == 0)
    def _():
        lax.fori_loop(0, GROUPS, first, 0)

    def relay_step(i):
        @pl.when(relay)
        def _():
            remote(gch[i].at[mine], gch[i].at[mine], ps_s.at[i], ps_r.at[i], zflip).wait_recv()
            pass_on(i).start()

    relay_step(0)
    for i in range(CHUNKS):
        if i + 1 < RELAYED:
            relay_step(i + 1)
        if i == 1:
            relay_row(0, range(GROUPS))
            pl.when(three)(lambda: relay_step(2))
        if i == 2:
            relay_row(1, range(GROUPS - 1))
        if i < 2:
            @pl.when(begin_mid & (three if i else jnp.logical_not(three)))
            def _():
                pl.when(x > 0)(share_right)
                start_exchange()

        @pl.when(early)
        def _(i=i):
            @pl.when(relay & (three if i >= RELAYED else True))
            def _():
                pass_on(i).wait_send()
                keep(i)[1].start()

            compute_sigma(i)

        @pl.when(needed)
        def _(i=i):
            for d in (1, 3, 2):
                y_send(0, i, d).start()
            side_own(i).start()

        if i == 2:
            relay_row(1, (GROUPS - 1,))
        if i == 0:
            pl.when(early & (x > 0))(lambda: start_lesser(2))
            pl.when(split & (x > 0))(lambda: start_greater(2))
        elif i == 1:
            pl.when(early & straight)(lambda: start_greater(2))
        else:
            pl.when((x > 0) & jnp.logical_not(begin_mid))(share_right)

        @pl.when(other_needed)
        def _(i=i):
            hop_in(i).wait_recv()
            for d in (1, 3, 2):
                y_send(1, i, d).start()
            side_send(other_col, i).start()

        if i:
            gathered(i - 1)
    gathered(CHUNKS - 1)
    pl.when(begin_end & (x > 0))(start_exchange)

    def both(g, carry):
        @pl.when(x > 0)
        def _():
            first(g, 0)

        return second(g, carry)

    lax.fori_loop(0, GROUPS, both, 0)

    @pl.when(x == 1)
    def _():
        for g in range(GROUPS):
            for q in range(2):
                sol_send(q, g, 2).start()

    pl.when(begin_end & (x == 0))(start_exchange)

    @pl.when(late)
    def _():
        @pl.when(relay)
        def _():
            for i in range(RELAYED):
                pass_on(i).wait_send()
                keep(i)[1].start()

        @pl.when(relay & three)
        def _():
            pass_on(RELAYED).wait_send()
            keep(RELAYED)[1].start()

        for i in range(CHUNKS):
            compute_sigma(i)

    for i in range(CHUNKS):
        exchange(i)[0].wait_send()
        if i < RELAYED:
            pl.when(split)(lambda i=i: pass_out(i).wait_send())
            pl.when(straight)(lambda i=i: exchange(i)[1].wait_send())
        else:
            pl.when(split & three)(lambda i=i: pass_out(i).wait_send())
            pl.when(jnp.logical_not(split & three))(lambda i=i: exchange(i)[1].wait_send())
        for q in range(2):
            sigma_out(i, q).wait()

        @pl.when(needed)
        def _(i=i):
            hop(i).wait_send()
            for d in (1, 2, 3):
                y_send(0, i, d).wait_send()
            side_own(i).wait_send()

        @pl.when(other_needed)
        def _(i=i):
            for d in (1, 2, 3):
                y_send(1, i, d).wait_send()
            side_send(other_col, i).wait_send()

        for d in (1, 2, 3):
            for half in range(2):
                j = half * 4 + (y + d) % 4

                @pl.when(j < row)
                def _(j=j, i=i):
                    side_send(j, i).wait_send()
    for m in range(2):
        for g in range(GROUPS):
            pl.when(jnp.logical_not(right_self(m)))(lambda m=m, g=g: right_send(m, g).wait_send())
    for q in range(2):
        diag_send(q).wait_send()
    for g in range(GROUPS):
        for q in range(2):
            pl.when(x < 3)(lambda q=q, g=g: sol_send(q, g, 1).wait_send())
            pl.when(x == 1)(lambda q=q, g=g: sol_send(q, g, 2).wait_send())
            pl.when(x == 0)(lambda q=q, g=g: sol_send(q, g, 3).wait_send())
            pl.when(last)(lambda q=q, g=g: row_on(q, g).wait_send())
            pl.when(jnp.logical_not(out_self(q)))(lambda q=q, g=g: out_send(q, g).wait_send())
        for m in range(2):
            from_self = jnp.logical_and(core == zl, zl == m)

            @pl.when(from_self)
            def _(m=m, g=g):
                pltpu.make_async_copy(obuf.at[0, g], out_tile(m, g), or_.at[m, g]).wait()

            @pl.when(jnp.logical_not(from_self))
            def _(m=m, g=g):
                remote(obuf.at[0, g], out_tile(m, g), os_.at[0, g], or_.at[m, g], sibling).wait_recv()


def on_device(lesser, greater, triples, diag_inverse, right_side):
    bf16, f32 = jnp.bfloat16, jnp.float32
    dma = pltpu.SemaphoreType.DMA
    hbm = pl.BlockSpec(memory_space=pl.ANY)
    sigma, solved = pl.pallas_call(
        kernel,
        out_shape=(
            jax.ShapeDtypeStruct(lesser.shape, bf16),
            jax.ShapeDtypeStruct(right_side.shape, bf16),
        ),
        in_specs=[pl.BlockSpec(memory_space=pltpu.SMEM), hbm, hbm, hbm, hbm],
        out_specs=(hbm, hbm),
        scratch_shapes=[pltpu.VMEM((4, 2, PART, SIDE), bf16) for _ in range(CHUNKS)]
        + [pltpu.VMEM((4, 2, SIDE, PART), bf16) for _ in range(CHUNKS)]
        + [
            pltpu.VMEM((4, 2, PART, SIDE), bf16),
            pltpu.VMEM((2, SIDE, WIDE), bf16),
            pltpu.VMEM((2, 8, SIDE, WIDE), bf16),
            pltpu.VMEM((2, SIDE, WIDE), bf16),
            pltpu.VMEM((2, GROUPS, SIDE, 2 * LANES), bf16),
            pltpu.VMEM((GROUPS, 2, SIDE, 2 * LANES), f32),
            pltpu.VMEM((8, GROUPS, 2, SIDE, LANES), bf16),
            pltpu.VMEM((2, GROUPS, SIDE, 2, LANES), bf16),
            pltpu.VMEM((2, SIDE, 2, SIDE), bf16),
            pltpu.VMEM((2, GROUPS, SIDE, 2 * LANES), bf16),
            dma((CHUNKS, 2)), dma((CHUNKS, 2)), dma((CHUNKS,)), dma((CHUNKS,)), dma((CHUNKS, 2)),
            dma((CHUNKS,)), dma((CHUNKS,)),
            dma((2, CHUNKS, 3)), dma((8, CHUNKS)),
            dma((8, CHUNKS)), dma((8, CHUNKS)),
            dma((2, GROUPS)), dma((2, GROUPS)),
            dma((2,)), dma((2,)), dma((2,)),
            dma((2, GROUPS, 3)), dma((8, GROUPS)),
            dma((2, GROUPS)), dma((2, GROUPS)),
            dma((CHUNKS, 2)), dma((1,)),
        ],
        compiler_params=pltpu.CompilerParams(
            collective_id=0, has_side_effects=True, vmem_limit_bytes=56 * 1024 * 1024
        ),
        name="second_born",
    )(triples.transpose(2, 0, 1), lesser, greater, diag_inverse, right_side)
    return (sigma, solved)


def solution(mesh):
    placed = (
        P("mom", None, "row", "col"),
        P("mom", None, "col", "row"),
        P(),
        P("mom", None, "row", None),
        P("mom", "row", None, "col"),
    )
    return jax.shard_map(
        on_device,
        mesh=mesh,
        in_specs=placed,
        out_specs=(P("mom", None, "row", "col"), P("mom", "row", None, "col")),
        check_vma=False,
    )
```

```python
import math

import jax
import jax.numpy as jnp
from jax import lax
from jax.experimental import pallas as pl
from jax.experimental.pallas import tpu as pltpu
from jax.sharding import PartitionSpec as P

MESH = pl.DeviceIdType.MESH
SIDE = 384
WIDE = 2 * SIDE
CHUNKS = 3
PART = SIDE // CHUNKS
GROUPS = 3
LANES = 128
PAIRS = 8
SUB = 16


def expand(real, imag):
    tall = jnp.concatenate([real, imag], axis=1)
    turned = jnp.concatenate([-imag, real], axis=1)
    return jnp.concatenate([tall, turned], axis=0)


def kernel(
    triples, lesser, greater, diag, right,
    sigma, solved,
    l0, l1, l2, g0, g1, g2, partner, own_sigma, rows_of, dbuf, rbuf, acc, sol, obuf, raw, plan,
    ex_s, ex_r, ps_s, ps_r, loc, zs, zr, ys, yr, ss, sr, rs, rr, dl, ds_, dr, xs, xr, os_, or_, out_s, raw_s,
):
    lch, gch = (l0, l1, l2), (g0, g1, g2)
    row = lax.axis_index("row")
    col = lax.axis_index("col")
    mom = lax.axis_index("mom")
    x, core = row // 2, row % 2
    zl, y = col // 4, col % 4
    weight = 1.0 / math.sqrt(SIDE * 8)

    def at(x_, core_, y_, zl_):
        return (x_ * 2 + core_, zl_ * 4 + y_, mom)

    pair_dev = (row, col, 1 - mom)
    sibling = at(x, 1 - core, y, zl)
    zflip = at(x, core, y, 1 - zl)

    def y_dev(d):
        return at(x, core, (y + d) % 4, zl)

    def x_dev(d):
        return at(x + d, core, y, zl)

    def remote(src, dst, send, recv, dev):
        return pltpu.make_async_remote_copy(
            src_ref=src, dst_ref=dst, send_sem=send, recv_sem=recv, device_id=dev, device_id_type=MESH
        )

    barrier = pltpu.get_barrier_semaphore()
    peers = [pair_dev, sibling, zflip, at(x, 1 - core, y, 1 - zl), (row, (1 - zl) * 4 + y, 1 - mom)]
    peers += [y_dev(d) for d in (1, 2, 3)]
    peers += [at((x + d) % 4, core, y, zl) for d in (1, 2, 3)]
    for peer in peers:
        pl.semaphore_signal(barrier, inc=1, device_id=peer, device_id_type=MESH)
    pl.semaphore_wait(barrier, len(peers))

    needed = col < row
    last = x == 3
    ring = y < 2 * x + 1
    early = jnp.logical_or(needed, last)
    late = jnp.logical_not(early)
    source = (y < row) & jnp.logical_not(last) & ((row != 5) | (y != 0))
    split = jnp.logical_and(source, zl == 0)
    relay = jnp.logical_and(source, zl == 1)
    straight = jnp.logical_not(split)
    begin_now = jnp.logical_and(late, jnp.logical_not(ring))
    begin_mid = late & relay & ((x != 2) | (y != 0))
    begin_end = late & ring & jnp.logical_not(begin_mid)
    three = ((x == 2) & (y == 0)) | ((x == 1) & (core == 0))
    pass_dev = (row, (1 - zl) * 4 + y, 1 - mom)

    def part(i):
        return pl.ds(i * PART, PART)

    mine = pl.ds(2 * mom, 2)

    def exchange(i):
        return (
            remote(lesser.at[:, :, part(i), :], lch[i].at[mine], ex_s.at[i, 0], ex_r.at[i, 0], pair_dev),
            remote(greater.at[:, :, :, part(i)], gch[i].at[mine], ex_s.at[i, 1], ex_r.at[i, 1], pair_dev),
        )

    def keep(i):
        return (
            pltpu.make_async_copy(lesser.at[:, :, part(i), :], lch[i].at[mine], loc.at[i, 0]),
            pltpu.make_async_copy(greater.at[:, :, :, part(i)], gch[i].at[mine], loc.at[i, 1]),
        )

    def right_self(m):
        return jnp.logical_and(core == zl, zl == m)

    def right_send(m, g):
        return remote(plan.at[m, g], rbuf.at[core, g], rs.at[m, g], rr.at[core, g], at(x, zl, y, m))

    def right_keep(m, g):
        return pltpu.make_async_copy(plan.at[m, g], rbuf.at[core, g], rr.at[core, g])

    def share_right():
        for g in range(GROUPS):
            for m in range(2):
                pl.when(right_self(m))(lambda m=m: right_keep(m, g).start())
                pl.when(jnp.logical_not(right_self(m)))(lambda m=m: right_send(m, g).start())

    raw_in = pltpu.make_async_copy(right, raw, raw_s.at[0])
    raw_in.start()

    def turn_right():
        raw_in.wait()

        def turn_group(t, carry):
            m, g = t // GROUPS, t % GROUPS
            lanes = pl.ds(pl.multiple_of(g * LANES, LANES), LANES)
            both_parts = raw[m, :, :, lanes].astype(jnp.float32)
            for c in range(2):
                plan[m, g, :, c * LANES : (c + 1) * LANES] = both_parts[:, c, :].astype(jnp.bfloat16)
            return carry

        lax.fori_loop(0, 2 * GROUPS, turn_group, 0)

    def start_exchange():
        for i in range(CHUNKS):
            for copy in exchange(i):
                copy.start()

    theirs = pl.ds(2 * (1 - mom), 2)

    def pass_out(i):
        return remote(
            greater.at[:, :, :, part(i)], gch[i].at[theirs], ex_s.at[i, 1], ps_r.at[i], pass_dev
        )

    def pass_on(i):
        return remote(gch[i].at[mine], gch[i].at[theirs], ps_s.at[i], ex_r.at[i, 1], zflip)

    def start_lesser(i):
        exchange(i)[0].start()

    RELAYED = 2

    def start_greater(i):
        if i < RELAYED:
            pl.when(split)(lambda: pass_out(i).start())
            pl.when(straight)(lambda: exchange(i)[1].start())
        else:
            pl.when(jnp.logical_not(split & three))(lambda: exchange(i)[1].start())

    @pl.when(early)
    def _():
        for i in (0, 1):
            start_lesser(i)
            start_greater(i)

        pl.when(split & three)(lambda: pass_out(2).start())

        @pl.when(x == 0)
        def _():
            start_lesser(2)
            start_greater(2)

    turn_right()
    pl.when(x == 0)(share_right)
    pl.when(begin_now)(start_exchange)

    def diag_keep(q):
        return pltpu.make_async_copy(diag.at[zl, q], dbuf.at[core, :, pl.ds(q * SIDE, SIDE)], dl.at[q])

    def diag_send(q):
        return remote(
            diag.at[zl, q], dbuf.at[core, :, pl.ds(q * SIDE, SIDE)], ds_.at[q], dr.at[q], sibling
        )

    for q in range(2):
        diag_keep(q).start()
        diag_send(q).start()
    for i in range(CHUNKS):
        keep(i)[0].start()
        if i < RELAYED:
            pl.when(jnp.logical_not(relay))(lambda i=i: keep(i)[1].start())
        else:
            pl.when(jnp.logical_not(relay & three))(lambda i=i: keep(i)[1].start())

    def sigma_out(i, q):
        return pltpu.make_async_copy(
            own_sigma.at[:, part(i), pl.ds(q * SIDE, SIDE)], sigma.at[:, q, part(i), :], out_s.at[i, q]
        )

    def compute_sigma(i):
        for copy in exchange(i):
            copy.wait_recv()
        for copy in keep(i):
            copy.wait()

        def turn(k, carry):
            for q in range(2):
                for b in range(3):
                    rows = pl.ds(b * LANES, LANES)
                    partner[k, q, :, rows] = gch[i][k, q, rows, :].T
            return carry

        lax.fori_loop(0, 4, turn, 0)

        def block(m, s, carry):
            here = pl.ds(pl.multiple_of(s * SUB, SUB), SUB)
            there = pl.ds(pl.multiple_of(i * PART + s * SUB, SUB), SUB)
            sum_real = jnp.zeros((SUB, SIDE), jnp.float32)
            sum_imag = jnp.zeros((SUB, SIDE), jnp.float32)
            for p in range(PAIRS):
                a, b, c = (triples[n, 2 * mom + m, p] for n in range(3))
                ar = lch[i][a, 0, here, :].astype(jnp.float32)
                ai = lch[i][a, 1, here, :].astype(jnp.float32)
                br = lch[i][b, 0, here, :].astype(jnp.float32)
                bi = lch[i][b, 1, here, :].astype(jnp.float32)
                cr = partner[c, 0, here, :].astype(jnp.float32)
                ci = partner[c, 1, here, :].astype(jnp.float32)
                pr = ar * br - ai * bi
                pi = ar * bi + ai * br
                sum_real += pr * cr - pi * ci
                sum_imag += pr * ci + pi * cr
            sig_real = (sum_real * (1.0 / PAIRS)).astype(jnp.bfloat16)
            sig_imag = (sum_imag * (1.0 / PAIRS)).astype(jnp.bfloat16)
            own_sigma[m, there, 0:SIDE] = sig_real
            own_sigma[m, there, SIDE:WIDE] = sig_imag

            @pl.when(zl == m)
            def _():
                rows_of[core, col, there, 0:SIDE] = sig_real
                rows_of[core, col, there, SIDE:WIDE] = sig_imag
            return carry

        lax.fori_loop(0, PART // SUB, lambda s, c: block(1 - zl, s, c), 0)
        pl.when(needed)(lambda: hop(i).start())
        lax.fori_loop(0, PART // SUB, lambda s, c: block(zl, s, c), 0)
        for q in range(2):
            sigma_out(i, q).start()

    def hop(i):
        return remote(
            own_sigma.at[1 - zl, part(i), :], rows_of.at[core, col, part(i), :], zs.at[i], zr.at[i], zflip
        )

    other_col = (1 - zl) * 4 + y
    other_needed = other_col < row

    def hop_in(i):
        tile = rows_of.at[core, other_col, part(i), :]
        return remote(tile, tile, zs.at[i], zr.at[i], zflip)

    def y_send(t, i, d):
        j = col if t == 0 else other_col
        src = own_sigma.at[zl, part(i), :] if t == 0 else rows_of.at[core, j, part(i), :]
        return remote(src, rows_of.at[core, j, part(i), :], ys.at[t, i, d - 1], yr.at[j, i], y_dev(d))

    def side_send(j, i):
        tile = rows_of.at[core, j, part(i), :]
        return remote(tile, tile, ss.at[j, i], sr.at[j, i], sibling)

    def side_own(i):
        return remote(
            own_sigma.at[zl, part(i), :], rows_of.at[core, col, part(i), :], ss.at[col, i], sr.at[col, i], sibling
        )

    def side_in(j, i):
        tile = rows_of.at[1 - core, j, part(i), :]
        return remote(tile, tile, ss.at[j, i], sr.at[j, i], sibling)

    def gathered(i):
        for d in (1, 2, 3):
            for half in range(2):
                j = half * 4 + (y + d) % 4

                @pl.when(j < row)
                def _(j=j):
                    tile = rows_of.at[core, j, part(i), :]
                    remote(tile, tile, ss.at[j, i], yr.at[j, i], sibling).wait_recv()
                    side_send(j, i).start()

    for q in range(2):
        diag_keep(q).wait()
        dst = dbuf.at[1 - core, :, pl.ds(q * SIDE, SIDE)]
        remote(diag.at[zl, q], dst, ds_.at[q], dr.at[q], sibling).wait_recv()
    def take_right(g):
        for q in range(2):
            from_self = jnp.logical_and(core == q, zl == core)

            @pl.when(from_self)
            def _(q=q):
                pltpu.make_async_copy(plan.at[0, g], rbuf.at[q, g], rr.at[q, g]).wait()

            @pl.when(jnp.logical_not(from_self))
            def _(q=q):
                remote(plan.at[0, g], rbuf.at[q, g], rs.at[0, g], rr.at[q, g], sibling).wait_recv()

    def sol_send(q, g, d):
        tile = sol.at[2 * x + q, g]
        return remote(tile, tile, xs.at[q, g, d - 1], xr.at[2 * x + q, g], x_dev(d))

    def out_self(q):
        return jnp.logical_and(core == q, zl == core)

    def out_tile(m, g):
        start = g * LANES if isinstance(g, int) else pl.multiple_of(g * LANES, LANES)
        return solved.at[m, :, :, pl.ds(start, LANES)]

    def out_send(q, g):
        return remote(
            obuf.at[q, g], out_tile(zl, g), os_.at[q, g], or_.at[zl, g], at(x, q, y, core)
        )

    def out_keep(q, g):
        return pltpu.make_async_copy(obuf.at[q, g], out_tile(zl, g), or_.at[zl, g])

    def side_wait(j, which):
        @pl.when(core != which)
        def _():
            for i in range(CHUNKS):
                side_in(j, i).wait_recv()

    def add_right(q, g):
        acc[g, q] += rbuf[q, g].astype(jnp.float32)

    def solve(q, g):
        pending = acc[g, q].astype(jnp.bfloat16)
        answer = jnp.dot(
            dbuf[q], expand(pending[:, :LANES], pending[:, LANES:]), preferred_element_type=jnp.float32
        ).astype(jnp.bfloat16)
        real, imag = answer[:, :LANES], answer[:, LANES:]
        sol[2 * x + q, g, 0] = real
        sol[2 * x + q, g, 1] = imag
        pl.when(x < 3)(lambda: sol_send(q, g, 1).start())
        pl.when(x == 0)(lambda: sol_send(q, g, 3).start())
        obuf[q, g] = jnp.stack([real, imag], axis=1)
        pl.when(out_self(q))(lambda: out_keep(q, g).start())
        pl.when(jnp.logical_not(out_self(q)))(lambda: out_send(q, g).start())

    def row_on(j, g):
        tile = sol.at[j, g]
        return remote(tile, tile, xs.at[j, g, 0], xr.at[j, g], x_dev(-1))

    def relay_row(j, groups):
        @pl.when(last)
        def _():
            for g in groups:
                row_on(j, g).wait_recv()
                row_on(j, g).start()

    def first(g, carry):
        acc[g] = jnp.zeros(acc.shape[1:], jnp.float32)

        def update(step, c):
            for t in range(2):
                j = 2 * step + t
                tile = sol.at[j, g]

                @pl.when(jnp.logical_not(last) | (j > 1))
                def _(tile=tile, j=j):
                    remote(tile, tile, xs.at[0, g, 0], xr.at[j, g], sibling).wait_recv()

                @pl.when(g == 0)
                def _(j=j):
                    side_wait(j, 0)
                    side_wait(j, 1)

                factor = expand(sol[j, g, 0], sol[j, g, 1])
                for q in range(2):
                    acc[g, q] += weight * jnp.dot(
                        rows_of[q, j], factor, preferred_element_type=jnp.float32
                    )
            return c

        lax.fori_loop(0, x, update, 0)
        take_right(g)
        for q in range(2):
            add_right(q, g)
        solve(0, g)
        return carry

    def second(g, carry):
        @pl.when(g == 0)
        def _():
            side_wait(2 * x, 1)

        acc[g, 1] += weight * jnp.dot(
            rows_of[1, 2 * x], expand(sol[2 * x, g, 0], sol[2 * x, g, 1]), preferred_element_type=jnp.float32
        )
        solve(1, g)
        return carry

    @pl.when(x == 0)
    def _():
        lax.fori_loop(0, GROUPS, first, 0)

    def relay_step(i):
        @pl.when(relay)
        def _():
            remote(gch[i].at[mine], gch[i].at[mine], ps_s.at[i], ps_r.at[i], zflip).wait_recv()
            pass_on(i).start()

    relay_step(0)
    for i in range(CHUNKS):
        if i + 1 < RELAYED:
            relay_step(i + 1)
        if i == 1:
            relay_row(0, range(GROUPS))
            pl.when(three)(lambda: relay_step(2))
        if i == 2:
            relay_row(1, range(GROUPS - 1))
        if i < 2:
            @pl.when(begin_mid & (three if i else jnp.logical_not(three)))
            def _():
                pl.when(x > 0)(share_right)
                start_exchange()

        @pl.when(early)
        def _(i=i):
            @pl.when(relay & (three if i >= RELAYED else True))
            def _():
                pass_on(i).wait_send()
                keep(i)[1].start()

            compute_sigma(i)

        @pl.when(needed)
        def _(i=i):
            for d in (1, 3, 2):
                y_send(0, i, d).start()
            side_own(i).start()

        if i == 2:
            relay_row(1, (GROUPS - 1,))
        if i == 0:
            pl.when(early & (x > 0))(lambda: start_lesser(2))
            pl.when(split & (x > 0))(lambda: start_greater(2))
        elif i == 1:
            pl.when(early & straight)(lambda: start_greater(2))
        else:
            pl.when((x > 0) & jnp.logical_not(begin_mid))(share_right)

        @pl.when(other_needed)
        def _(i=i):
            hop_in(i).wait_recv()
            for d in (1, 3, 2):
                y_send(1, i, d).start()
            side_send(other_col, i).start()

        if i:
            gathered(i - 1)
    gathered(CHUNKS - 1)
    pl.when(begin_end & (x > 0))(start_exchange)

    def both(g, carry):
        @pl.when(x > 0)
        def _():
            first(g, 0)

        return second(g, carry)

    lax.fori_loop(0, GROUPS, both, 0)

    @pl.when(x == 1)
    def _():
        for g in range(GROUPS):
            for q in range(2):
                sol_send(q, g, 2).start()

    pl.when(begin_end & (x == 0))(start_exchange)

    @pl.when(late)
    def _():
        @pl.when(relay)
        def _():
            for i in range(RELAYED):
                pass_on(i).wait_send()
                keep(i)[1].start()

        @pl.when(relay & three)
        def _():
            pass_on(RELAYED).wait_send()
            keep(RELAYED)[1].start()

        for i in range(CHUNKS):
            compute_sigma(i)

    for i in range(CHUNKS):
        exchange(i)[0].wait_send()
        if i < RELAYED:
            pl.when(split)(lambda i=i: pass_out(i).wait_send())
            pl.when(straight)(lambda i=i: exchange(i)[1].wait_send())
        else:
            pl.when(split & three)(lambda i=i: pass_out(i).wait_send())
            pl.when(jnp.logical_not(split & three))(lambda i=i: exchange(i)[1].wait_send())
        for q in range(2):
            sigma_out(i, q).wait()

        @pl.when(needed)
        def _(i=i):
            hop(i).wait_send()
            for d in (1, 2, 3):
                y_send(0, i, d).wait_send()
            side_own(i).wait_send()

        @pl.when(other_needed)
        def _(i=i):
            for d in (1, 2, 3):
                y_send(1, i, d).wait_send()
            side_send(other_col, i).wait_send()

        for d in (1, 2, 3):
            for half in range(2):
                j = half * 4 + (y + d) % 4

                @pl.when(j < row)
                def _(j=j, i=i):
                    side_send(j, i).wait_send()
    for m in range(2):
        for g in range(GROUPS):
            pl.when(jnp.logical_not(right_self(m)))(lambda m=m, g=g: right_send(m, g).wait_send())
    for q in range(2):
        diag_send(q).wait_send()
    for g in range(GROUPS):
        for q in range(2):
            pl.when(x < 3)(lambda q=q, g=g: sol_send(q, g, 1).wait_send())
            pl.when(x == 1)(lambda q=q, g=g: sol_send(q, g, 2).wait_send())
            pl.when(x == 0)(lambda q=q, g=g: sol_send(q, g, 3).wait_send())
            pl.when(last)(lambda q=q, g=g: row_on(q, g).wait_send())
            pl.when(jnp.logical_not(out_self(q)))(lambda q=q, g=g: out_send(q, g).wait_send())
        for m in range(2):
            from_self = jnp.logical_and(core == zl, zl == m)

            @pl.when(from_self)
            def _(m=m, g=g):
                pltpu.make_async_copy(obuf.at[0, g], out_tile(m, g), or_.at[m, g]).wait()

            @pl.when(jnp.logical_not(from_self))
            def _(m=m, g=g):
                remote(obuf.at[0, g], out_tile(m, g), os_.at[0, g], or_.at[m, g], sibling).wait_recv()


def on_device(lesser, greater, triples, diag_inverse, right_side):
    bf16, f32 = jnp.bfloat16, jnp.float32
    dma = pltpu.SemaphoreType.DMA
    hbm = pl.BlockSpec(memory_space=pl.ANY)
    sigma, solved = pl.pallas_call(
        kernel,
        out_shape=(
            jax.ShapeDtypeStruct(lesser.shape, bf16),
            jax.ShapeDtypeStruct(right_side.shape, bf16),
        ),
        in_specs=[pl.BlockSpec(memory_space=pltpu.SMEM), hbm, hbm, hbm, hbm],
        out_specs=(hbm, hbm),
        scratch_shapes=[pltpu.VMEM((4, 2, PART, SIDE), bf16) for _ in range(CHUNKS)]
        + [pltpu.VMEM((4, 2, SIDE, PART), bf16) for _ in range(CHUNKS)]
        + [
            pltpu.VMEM((4, 2, PART, SIDE), bf16),
            pltpu.VMEM((2, SIDE, WIDE), bf16),
            pltpu.VMEM((2, 8, SIDE, WIDE), bf16),
            pltpu.VMEM((2, SIDE, WIDE), bf16),
            pltpu.VMEM((2, GROUPS, SIDE, 2 * LANES), bf16),
            pltpu.VMEM((GROUPS, 2, SIDE, 2 * LANES), f32),
            pltpu.VMEM((8, GROUPS, 2, SIDE, LANES), bf16),
            pltpu.VMEM((2, GROUPS, SIDE, 2, LANES), bf16),
            pltpu.VMEM((2, SIDE, 2, SIDE), bf16),
            pltpu.VMEM((2, GROUPS, SIDE, 2 * LANES), bf16),
            dma((CHUNKS, 2)), dma((CHUNKS, 2)), dma((CHUNKS,)), dma((CHUNKS,)), dma((CHUNKS, 2)),
            dma((CHUNKS,)), dma((CHUNKS,)),
            dma((2, CHUNKS, 3)), dma((8, CHUNKS)),
            dma((8, CHUNKS)), dma((8, CHUNKS)),
            dma((2, GROUPS)), dma((2, GROUPS)),
            dma((2,)), dma((2,)), dma((2,)),
            dma((2, GROUPS, 3)), dma((8, GROUPS)),
            dma((2, GROUPS)), dma((2, GROUPS)),
            dma((CHUNKS, 2)), dma((1,)),
        ],
        compiler_params=pltpu.CompilerParams(
            collective_id=0, has_side_effects=True, vmem_limit_bytes=51 * 1024 * 1024
        ),
        name="second_born",
    )(triples.transpose(2, 0, 1), lesser, greater, diag_inverse, right_side)
    return (sigma, solved)


def solution(mesh):
    placed = (
        P("mom", None, "row", "col"),
        P("mom", None, "col", "row"),
        P(),
        P("mom", None, "row", None),
        P("mom", "row", None, "col"),
    )
    return jax.shard_map(
        on_device,
        mesh=mesh,
        in_specs=placed,
        out_specs=(P("mom", None, "row", "col"), P("mom", "row", None, "col")),
        check_vma=False,
    )
```

```python
import math

import jax
import jax.numpy as jnp
from jax import lax
from jax.experimental import pallas as pl
from jax.experimental.pallas import tpu as pltpu
from jax.sharding import PartitionSpec as P

MESH = pl.DeviceIdType.MESH
SIDE = 384
WIDE = 2 * SIDE
CHUNKS = 3
PART = SIDE // CHUNKS
GROUPS = 3
LANES = 128
PAIRS = 8
SUB = 16


def expand(real, imag):
    tall = jnp.concatenate([real, imag], axis=1)
    turned = jnp.concatenate([-imag, real], axis=1)
    return jnp.concatenate([tall, turned], axis=0)


def kernel(
    triples, lesser, greater, diag, right,
    sigma, solved,
    l0, l1, l2, g0, g1, g2, partner, own_sigma, rows_of, dbuf, rbuf, acc, sol, obuf, raw, plan,
    ex_s, ex_r, ps_s, ps_r, loc, zs, zr, ys, yr, ss, sr, rs, rr, dl, ds_, dr, xs, xr, os_, or_, out_s, raw_s,
):
    lch, gch = (l0, l1, l2), (g0, g1, g2)
    row = lax.axis_index("row")
    col = lax.axis_index("col")
    mom = lax.axis_index("mom")
    x, core = row // 2, row % 2
    zl, y = col // 4, col % 4
    weight = 1.0 / math.sqrt(SIDE * 8)

    def at(x_, core_, y_, zl_):
        return (x_ * 2 + core_, zl_ * 4 + y_, mom)

    pair_dev = (row, col, 1 - mom)
    sibling = at(x, 1 - core, y, zl)
    zflip = at(x, core, y, 1 - zl)

    def y_dev(d):
        return at(x, core, (y + d) % 4, zl)

    def x_dev(d):
        return at(x + d, core, y, zl)

    def remote(src, dst, send, recv, dev):
        return pltpu.make_async_remote_copy(
            src_ref=src, dst_ref=dst, send_sem=send, recv_sem=recv, device_id=dev, device_id_type=MESH
        )

    barrier = pltpu.get_barrier_semaphore()
    peers = [pair_dev, sibling, zflip, at(x, 1 - core, y, 1 - zl), (row, (1 - zl) * 4 + y, 1 - mom)]
    peers += [y_dev(d) for d in (1, 2, 3)]
    peers += [at((x + d) % 4, core, y, zl) for d in (1, 2, 3)]
    for peer in peers:
        pl.semaphore_signal(barrier, inc=1, device_id=peer, device_id_type=MESH)
    pl.semaphore_wait(barrier, len(peers))

    needed = col < row
    last = x == 3
    ring = y < 2 * x + 1
    early = jnp.logical_or(needed, last)
    late = jnp.logical_not(early)
    source = (y < row) & jnp.logical_not(last) & ((row != 5) | (y != 0))
    split = jnp.logical_and(source, zl == 0)
    relay = jnp.logical_and(source, zl == 1)
    straight = jnp.logical_not(split)
    begin_now = jnp.logical_and(late, jnp.logical_not(ring))
    begin_mid = late & relay & ((x != 2) | (y != 0))
    begin_end = late & ring & jnp.logical_not(begin_mid)
    three = ((x == 2) & (y == 0)) | ((x == 1) & (core == 0))
    pass_dev = (row, (1 - zl) * 4 + y, 1 - mom)

    def part(i):
        return pl.ds(i * PART, PART)

    mine = pl.ds(2 * mom, 2)

    def exchange(i):
        return (
            remote(lesser.at[:, :, part(i), :], lch[i].at[mine], ex_s.at[i, 0], ex_r.at[i, 0], pair_dev),
            remote(greater.at[:, :, :, part(i)], gch[i].at[mine], ex_s.at[i, 1], ex_r.at[i, 1], pair_dev),
        )

    def keep(i):
        return (
            pltpu.make_async_copy(lesser.at[:, :, part(i), :], lch[i].at[mine], loc.at[i, 0]),
            pltpu.make_async_copy(greater.at[:, :, :, part(i)], gch[i].at[mine], loc.at[i, 1]),
        )

    def right_self(m):
        return jnp.logical_and(core == zl, zl == m)

    def right_send(m, g):
        return remote(plan.at[m, g], rbuf.at[core, g], rs.at[m, g], rr.at[core, g], at(x, zl, y, m))

    def right_keep(m, g):
        return pltpu.make_async_copy(plan.at[m, g], rbuf.at[core, g], rr.at[core, g])

    def share_right():
        for g in range(GROUPS):
            for m in range(2):
                pl.when(right_self(m))(lambda m=m: right_keep(m, g).start())
                pl.when(jnp.logical_not(right_self(m)))(lambda m=m: right_send(m, g).start())

    raw_in = pltpu.make_async_copy(right, raw, raw_s.at[0])
    raw_in.start()

    def turn_right():
        raw_in.wait()

        def turn_group(t, carry):
            m, g = t // GROUPS, t % GROUPS
            lanes = pl.ds(pl.multiple_of(g * LANES, LANES), LANES)
            both_parts = raw[m, :, :, lanes].astype(jnp.float32)
            for c in range(2):
                plan[m, g, :, c * LANES : (c + 1) * LANES] = both_parts[:, c, :].astype(jnp.bfloat16)
            return carry

        lax.fori_loop(0, 2 * GROUPS, turn_group, 0)

    def start_exchange():
        for i in range(CHUNKS):
            for copy in exchange(i):
                copy.start()

    theirs = pl.ds(2 * (1 - mom), 2)

    def pass_out(i):
        return remote(
            greater.at[:, :, :, part(i)], gch[i].at[theirs], ex_s.at[i, 1], ps_r.at[i], pass_dev
        )

    def pass_on(i):
        return remote(gch[i].at[mine], gch[i].at[theirs], ps_s.at[i], ex_r.at[i, 1], zflip)

    def start_lesser(i):
        exchange(i)[0].start()

    RELAYED = 2

    def start_greater(i):
        if i < RELAYED:
            pl.when(split)(lambda: pass_out(i).start())
            pl.when(straight)(lambda: exchange(i)[1].start())
        else:
            pl.when(jnp.logical_not(split & three))(lambda: exchange(i)[1].start())

    @pl.when(early)
    def _():
        for i in (0, 1):
            start_lesser(i)
            start_greater(i)

        pl.when(split & three)(lambda: pass_out(2).start())

        @pl.when(x == 0)
        def _():
            start_lesser(2)
            start_greater(2)

    turn_right()
    pl.when(x == 0)(share_right)
    pl.when(begin_now)(start_exchange)

    def diag_keep(q):
        return pltpu.make_async_copy(diag.at[zl, q], dbuf.at[core, :, pl.ds(q * SIDE, SIDE)], dl.at[q])

    def diag_send(q):
        return remote(
            diag.at[zl, q], dbuf.at[core, :, pl.ds(q * SIDE, SIDE)], ds_.at[q], dr.at[q], sibling
        )

    for q in range(2):
        diag_keep(q).start()
        diag_send(q).start()
    for i in range(CHUNKS):
        keep(i)[0].start()
        if i < RELAYED:
            pl.when(jnp.logical_not(relay))(lambda i=i: keep(i)[1].start())
        else:
            pl.when(jnp.logical_not(relay & three))(lambda i=i: keep(i)[1].start())

    def sigma_out(i, q):
        return pltpu.make_async_copy(
            own_sigma.at[:, part(i), pl.ds(q * SIDE, SIDE)], sigma.at[:, q, part(i), :], out_s.at[i, q]
        )

    def compute_sigma(i):
        for copy in exchange(i):
            copy.wait_recv()
        for copy in keep(i):
            copy.wait()

        def turn(k, carry):
            for q in range(2):
                for b in range(3):
                    rows = pl.ds(b * LANES, LANES)
                    partner[k, q, :, rows] = gch[i][k, q, rows, :].T
            return carry

        lax.fori_loop(0, 4, turn, 0)

        def block(m, s, carry):
            here = pl.ds(pl.multiple_of(s * SUB, SUB), SUB)
            there = pl.ds(pl.multiple_of(i * PART + s * SUB, SUB), SUB)
            sum_real = jnp.zeros((SUB, SIDE), jnp.float32)
            sum_imag = jnp.zeros((SUB, SIDE), jnp.float32)
            for p in range(PAIRS):
                a, b, c = (triples[n, 2 * mom + m, p] for n in range(3))
                ar = lch[i][a, 0, here, :].astype(jnp.float32)
                ai = lch[i][a, 1, here, :].astype(jnp.float32)
                br = lch[i][b, 0, here, :].astype(jnp.float32)
                bi = lch[i][b, 1, here, :].astype(jnp.float32)
                cr = partner[c, 0, here, :].astype(jnp.float32)
                ci = partner[c, 1, here, :].astype(jnp.float32)
                pr = ar * br - ai * bi
                pi = ar * bi + ai * br
                sum_real += pr * cr - pi * ci
                sum_imag += pr * ci + pi * cr
            sig_real = (sum_real * (1.0 / PAIRS)).astype(jnp.bfloat16)
            sig_imag = (sum_imag * (1.0 / PAIRS)).astype(jnp.bfloat16)
            own_sigma[m, there, 0:SIDE] = sig_real
            own_sigma[m, there, SIDE:WIDE] = sig_imag

            @pl.when(zl == m)
            def _():
                rows_of[core, col, there, 0:SIDE] = sig_real
                rows_of[core, col, there, SIDE:WIDE] = sig_imag
            return carry

        lax.fori_loop(0, PART // SUB, lambda s, c: block(1 - zl, s, c), 0)
        pl.when(needed)(lambda: hop(i).start())
        lax.fori_loop(0, PART // SUB, lambda s, c: block(zl, s, c), 0)
        for q in range(2):
            sigma_out(i, q).start()

    def hop(i):
        return remote(
            own_sigma.at[1 - zl, part(i), :], rows_of.at[core, col, part(i), :], zs.at[i], zr.at[i], zflip
        )

    other_col = (1 - zl) * 4 + y
    other_needed = other_col < row

    def hop_in(i):
        tile = rows_of.at[core, other_col, part(i), :]
        return remote(tile, tile, zs.at[i], zr.at[i], zflip)

    def y_send(t, i, d):
        j = col if t == 0 else other_col
        src = own_sigma.at[zl, part(i), :] if t == 0 else rows_of.at[core, j, part(i), :]
        return remote(src, rows_of.at[core, j, part(i), :], ys.at[t, i, d - 1], yr.at[j, i], y_dev(d))

    def side_send(j, i):
        tile = rows_of.at[core, j, part(i), :]
        return remote(tile, tile, ss.at[j, i], sr.at[j, i], sibling)

    def side_own(i):
        return remote(
            own_sigma.at[zl, part(i), :], rows_of.at[core, col, part(i), :], ss.at[col, i], sr.at[col, i], sibling
        )

    def side_in(j, i):
        tile = rows_of.at[1 - core, j, part(i), :]
        return remote(tile, tile, ss.at[j, i], sr.at[j, i], sibling)

    def gathered(i):
        for d in (1, 2, 3):
            for half in range(2):
                j = half * 4 + (y + d) % 4

                @pl.when(j < row)
                def _(j=j):
                    tile = rows_of.at[core, j, part(i), :]
                    remote(tile, tile, ss.at[j, i], yr.at[j, i], sibling).wait_recv()
                    side_send(j, i).start()

    for q in range(2):
        diag_keep(q).wait()
        dst = dbuf.at[1 - core, :, pl.ds(q * SIDE, SIDE)]
        remote(diag.at[zl, q], dst, ds_.at[q], dr.at[q], sibling).wait_recv()
    def take_right(g):
        for q in range(2):
            from_self = jnp.logical_and(core == q, zl == core)

            @pl.when(from_self)
            def _(q=q):
                pltpu.make_async_copy(plan.at[0, g], rbuf.at[q, g], rr.at[q, g]).wait()

            @pl.when(jnp.logical_not(from_self))
            def _(q=q):
                remote(plan.at[0, g], rbuf.at[q, g], rs.at[0, g], rr.at[q, g], sibling).wait_recv()

    def sol_send(q, g, d):
        tile = sol.at[2 * x + q, g]
        return remote(tile, tile, xs.at[q, g, d - 1], xr.at[2 * x + q, g], x_dev(d))

    def out_self(q):
        return jnp.logical_and(core == q, zl == core)

    def out_tile(m, g):
        start = g * LANES if isinstance(g, int) else pl.multiple_of(g * LANES, LANES)
        return solved.at[m, :, :, pl.ds(start, LANES)]

    def out_send(q, g):
        return remote(
            obuf.at[q, g], out_tile(zl, g), os_.at[q, g], or_.at[zl, g], at(x, q, y, core)
        )

    def out_keep(q, g):
        return pltpu.make_async_copy(obuf.at[q, g], out_tile(zl, g), or_.at[zl, g])

    def side_wait(j, which):
        @pl.when(core != which)
        def _():
            for i in range(CHUNKS):
                side_in(j, i).wait_recv()

    def add_right(q, g):
        acc[g, q] += rbuf[q, g].astype(jnp.float32)

    def solve(q, g):
        pending = acc[g, q].astype(jnp.bfloat16)
        answer = jnp.dot(
            dbuf[q], expand(pending[:, :LANES], pending[:, LANES:]), preferred_element_type=jnp.float32
        ).astype(jnp.bfloat16)
        real, imag = answer[:, :LANES], answer[:, LANES:]
        sol[2 * x + q, g, 0] = real
        sol[2 * x + q, g, 1] = imag
        pl.when(x < 3)(lambda: sol_send(q, g, 1).start())
        pl.when(x == 0)(lambda: sol_send(q, g, 3).start())
        obuf[q, g] = jnp.stack([real, imag], axis=1)
        pl.when(out_self(q))(lambda: out_keep(q, g).start())
        pl.when(jnp.logical_not(out_self(q)))(lambda: out_send(q, g).start())

    def row_on(j, g):
        tile = sol.at[j, g]
        return remote(tile, tile, xs.at[j, g, 0], xr.at[j, g], x_dev(-1))

    def relay_row(j, groups):
        @pl.when(last)
        def _():
            for g in groups:
                row_on(j, g).wait_recv()
                row_on(j, g).start()

    def first(g, carry):
        acc[g] = jnp.zeros(acc.shape[1:], jnp.float32)

        def update(step, c):
            for t in range(2):
                j = 2 * step + t
                tile = sol.at[j, g]

                @pl.when(jnp.logical_not(last) | (j > 1))
                def _(tile=tile, j=j):
                    remote(tile, tile, xs.at[0, g, 0], xr.at[j, g], sibling).wait_recv()

                @pl.when(g == 0)
                def _(j=j):
                    side_wait(j, 0)
                    side_wait(j, 1)

                factor = expand(sol[j, g, 0], sol[j, g, 1])
                for q in range(2):
                    acc[g, q] += weight * jnp.dot(
                        rows_of[q, j], factor, preferred_element_type=jnp.float32
                    )
            return c

        lax.fori_loop(0, x, update, 0)
        take_right(g)
        for q in range(2):
            add_right(q, g)
        solve(0, g)
        return carry

    def second(g, carry):
        @pl.when(g == 0)
        def _():
            side_wait(2 * x, 1)

        acc[g, 1] += weight * jnp.dot(
            rows_of[1, 2 * x], expand(sol[2 * x, g, 0], sol[2 * x, g, 1]), preferred_element_type=jnp.float32
        )
        solve(1, g)
        return carry

    @pl.when(x == 0)
    def _():
        lax.fori_loop(0, GROUPS, first, 0)

    def relay_step(i):
        @pl.when(relay)
        def _():
            remote(gch[i].at[mine], gch[i].at[mine], ps_s.at[i], ps_r.at[i], zflip).wait_recv()
            pass_on(i).start()

    relay_step(0)
    for i in range(CHUNKS):
        if i + 1 < RELAYED:
            relay_step(i + 1)
        if i == 1:
            relay_row(0, range(GROUPS))
            pl.when(three)(lambda: relay_step(2))
        if i == 2:
            relay_row(1, range(GROUPS - 1))
        if i < 2:
            @pl.when(begin_mid & (three if i else jnp.logical_not(three)))
            def _():
                pl.when(x > 0)(share_right)
                start_exchange()

        @pl.when(early)
        def _(i=i):
            @pl.when(relay & (three if i >= RELAYED else True))
            def _():
                pass_on(i).wait_send()
                keep(i)[1].start()

            compute_sigma(i)

        @pl.when(needed)
        def _(i=i):
            for d in (2, 1, 3):
                y_send(0, i, d).start()
            side_own(i).start()

        if i == 2:
            relay_row(1, (GROUPS - 1,))
        if i == 0:
            pl.when(early & (x > 0))(lambda: start_lesser(2))
            pl.when(split & (x > 0))(lambda: start_greater(2))
        elif i == 1:
            pl.when(early & straight)(lambda: start_greater(2))
        else:
            pl.when((x > 0) & jnp.logical_not(begin_mid))(share_right)

        @pl.when(other_needed)
        def _(i=i):
            hop_in(i).wait_recv()
            for d in (2, 1, 3):
                y_send(1, i, d).start()
            side_send(other_col, i).start()

        if i:
            gathered(i - 1)
    gathered(CHUNKS - 1)
    pl.when(begin_end & (x > 0))(start_exchange)

    def both(g, carry):
        @pl.when(x > 0)
        def _():
            first(g, 0)

        return second(g, carry)

    lax.fori_loop(0, GROUPS, both, 0)

    @pl.when(x == 1)
    def _():
        for g in range(GROUPS):
            for q in range(2):
                sol_send(q, g, 2).start()

    pl.when(begin_end & (x == 0))(start_exchange)

    @pl.when(late)
    def _():
        @pl.when(relay)
        def _():
            for i in range(RELAYED):
                pass_on(i).wait_send()
                keep(i)[1].start()

        @pl.when(relay & three)
        def _():
            pass_on(RELAYED).wait_send()
            keep(RELAYED)[1].start()

        for i in range(CHUNKS):
            compute_sigma(i)

    for i in range(CHUNKS):
        exchange(i)[0].wait_send()
        if i < RELAYED:
            pl.when(split)(lambda i=i: pass_out(i).wait_send())
            pl.when(straight)(lambda i=i: exchange(i)[1].wait_send())
        else:
            pl.when(split & three)(lambda i=i: pass_out(i).wait_send())
            pl.when(jnp.logical_not(split & three))(lambda i=i: exchange(i)[1].wait_send())
        for q in range(2):
            sigma_out(i, q).wait()

        @pl.when(needed)
        def _(i=i):
            hop(i).wait_send()
            for d in (1, 2, 3):
                y_send(0, i, d).wait_send()
            side_own(i).wait_send()

        @pl.when(other_needed)
        def _(i=i):
            for d in (1, 2, 3):
                y_send(1, i, d).wait_send()
            side_send(other_col, i).wait_send()

        for d in (1, 2, 3):
            for half in range(2):
                j = half * 4 + (y + d) % 4

                @pl.when(j < row)
                def _(j=j, i=i):
                    side_send(j, i).wait_send()
    for m in range(2):
        for g in range(GROUPS):
            pl.when(jnp.logical_not(right_self(m)))(lambda m=m, g=g: right_send(m, g).wait_send())
    for q in range(2):
        diag_send(q).wait_send()
    for g in range(GROUPS):
        for q in range(2):
            pl.when(x < 3)(lambda q=q, g=g: sol_send(q, g, 1).wait_send())
            pl.when(x == 1)(lambda q=q, g=g: sol_send(q, g, 2).wait_send())
            pl.when(x == 0)(lambda q=q, g=g: sol_send(q, g, 3).wait_send())
            pl.when(last)(lambda q=q, g=g: row_on(q, g).wait_send())
            pl.when(jnp.logical_not(out_self(q)))(lambda q=q, g=g: out_send(q, g).wait_send())
        for m in range(2):
            from_self = jnp.logical_and(core == zl, zl == m)

            @pl.when(from_self)
            def _(m=m, g=g):
                pltpu.make_async_copy(obuf.at[0, g], out_tile(m, g), or_.at[m, g]).wait()

            @pl.when(jnp.logical_not(from_self))
            def _(m=m, g=g):
                remote(obuf.at[0, g], out_tile(m, g), os_.at[0, g], or_.at[m, g], sibling).wait_recv()


def on_device(lesser, greater, triples, diag_inverse, right_side):
    bf16, f32 = jnp.bfloat16, jnp.float32
    dma = pltpu.SemaphoreType.DMA
    hbm = pl.BlockSpec(memory_space=pl.ANY)
    sigma, solved = pl.pallas_call(
        kernel,
        out_shape=(
            jax.ShapeDtypeStruct(lesser.shape, bf16),
            jax.ShapeDtypeStruct(right_side.shape, bf16),
        ),
        in_specs=[pl.BlockSpec(memory_space=pltpu.SMEM), hbm, hbm, hbm, hbm],
        out_specs=(hbm, hbm),
        scratch_shapes=[pltpu.VMEM((4, 2, PART, SIDE), bf16) for _ in range(CHUNKS)]
        + [pltpu.VMEM((4, 2, SIDE, PART), bf16) for _ in range(CHUNKS)]
        + [
            pltpu.VMEM((4, 2, PART, SIDE), bf16),
            pltpu.VMEM((2, SIDE, WIDE), bf16),
            pltpu.VMEM((2, 8, SIDE, WIDE), bf16),
            pltpu.VMEM((2, SIDE, WIDE), bf16),
            pltpu.VMEM((2, GROUPS, SIDE, 2 * LANES), bf16),
            pltpu.VMEM((GROUPS, 2, SIDE, 2 * LANES), f32),
            pltpu.VMEM((8, GROUPS, 2, SIDE, LANES), bf16),
            pltpu.VMEM((2, GROUPS, SIDE, 2, LANES), bf16),
            pltpu.VMEM((2, SIDE, 2, SIDE), bf16),
            pltpu.VMEM((2, GROUPS, SIDE, 2 * LANES), bf16),
            dma((CHUNKS, 2)), dma((CHUNKS, 2)), dma((CHUNKS,)), dma((CHUNKS,)), dma((CHUNKS, 2)),
            dma((CHUNKS,)), dma((CHUNKS,)),
            dma((2, CHUNKS, 3)), dma((8, CHUNKS)),
            dma((8, CHUNKS)), dma((8, CHUNKS)),
            dma((2, GROUPS)), dma((2, GROUPS)),
            dma((2,)), dma((2,)), dma((2,)),
            dma((2, GROUPS, 3)), dma((8, GROUPS)),
            dma((2, GROUPS)), dma((2, GROUPS)),
            dma((CHUNKS, 2)), dma((1,)),
        ],
        compiler_params=pltpu.CompilerParams(
            collective_id=0, has_side_effects=True, vmem_limit_bytes=51 * 1024 * 1024
        ),
        name="second_born",
    )(triples.transpose(2, 0, 1), lesser, greater, diag_inverse, right_side)
    return (sigma, solved)


def solution(mesh):
    placed = (
        P("mom", None, "row", "col"),
        P("mom", None, "col", "row"),
        P(),
        P("mom", None, "row", None),
        P("mom", "row", None, "col"),
    )
    return jax.shard_map(
        on_device,
        mesh=mesh,
        in_specs=placed,
        out_specs=(P("mom", None, "row", "col"), P("mom", "row", None, "col")),
        check_vma=False,
    )
```
